32 devices in a mesh: dp: 8 (over z, core), tensor: 4 (over y, x).
Axes of the slice: x: 2, y: 2, z: 4, core: 2. Of those that a mesh axis runs over, the one named last changes fastest.
Arguments:
- tokens: bfloat16 [8192, 2048], P(('dp', 'tensor')), may hold values from -6 to 6
- cotangent: bfloat16 [8192, 2048], P(('dp', 'tensor')), may hold values from -6 to 6
- lengths: int32 [8], P('dp'), may hold values from 256 to 1024, as said below
- norm_gain: bfloat16 [2048], P('dp'), may hold values from 0.5 to 1.5
- norm_bias: bfloat16 [2048], P('dp'), may hold values from -1.75 to 1.75
- query_weight: bfloat16 [2048, 2048], P('dp', 'tensor'), may hold values from -0.125 to 0.125
- key_weight: bfloat16 [2048, 2048], P('dp', 'tensor'), may hold values from -0.125 to 0.125
- value_weight: bfloat16 [2048, 2048], P('dp', 'tensor'), may hold values from -0.125 to 0.125
- qkv_bias: bfloat16 [3, 32, 64], P(None, 'tensor', 'dp'), may hold values from -1.75 to 1.75
- proj_weight: bfloat16 [2048, 2048], P('tensor', 'dp'), may hold values from -1.5 to 1.5
- proj_bias: bfloat16 [2048], P('dp'), may hold values from -1.75 to 1.75
- up_weight: bfloat16 [2048, 8192], P('dp', 'tensor'), may hold values from -0.125 to 0.125
- up_bias: bfloat16 [128, 64], P('tensor', 'dp'), may hold values from -3 to 3
- down_weight: bfloat16 [8192, 2048], P('tensor', 'dp'), may hold values from -0.0625 to 0.0625
- down_bias: bfloat16 [2048], P('dp'), may hold values from -1.75 to 1.75
Outputs:
- output: bfloat16 [8192, 2048], P(('dp', 'tensor'))
- input_grad: float32 [8192, 2048], P(('dp', 'tensor'))
- norm_gain_grad: float32 [2048], P('dp')
- norm_bias_grad: float32 [2048], P('dp')
- query_grad: float32 [2048, 2048], P('dp', 'tensor')
- key_grad: float32 [2048, 2048], P('dp', 'tensor')
- value_grad: float32 [2048, 2048], P('dp', 'tensor')
- qkv_bias_grad: float32 [3, 32, 64], P(None, 'tensor', 'dp')
- proj_grad: float32 [2048, 2048], P('tensor', 'dp')
- proj_bias_grad: float32 [2048], P('dp')
- up_grad: float32 [2048, 8192], P('dp', 'tensor')
- up_bias_grad: float32 [128, 64], P('tensor', 'dp')
- down_grad: float32 [8192, 2048], P('tensor', 'dp')
- down_bias_grad: float32 [2048], P('dp')
The draws below stay inside these ranges and needn't reach their ends.
Inputs may be any that keep to these rules, and one draw needn't show every extreme that they name: `lengths`: each slot holds one sequence from its first row; in every draw some slot is full, of length 1024.
All inputs are finite; a program needn't handle non-finite values.
Results may differ from the reference program's by a relative error of at most 0.017.
Values may be sent and summed in bfloat16 or wider, within the bound.
No kernel may reach another device: no remote copies, remote signals or barrier semaphores. Data moves between devices by JAX's collectives and lax.ppermute only.
A program may use at most 192 MiB of HBM per device.

```python
import jax
import jax.numpy as jnp
from jax import lax

D = 2048
FF = 8192
HEADS = 32
HEAD = 64
ROT = 32
SLOT_LEN = 1024
MIN_LEN = 256
SLOTS = 8
TOKENS = 8192


def draw_lengths(key, part):
    first, second = jax.random.split(jax.random.fold_in(key, 11))
    values = jax.random.randint(first, (SLOTS,), MIN_LEN, SLOT_LEN + 1)
    chosen = jax.random.randint(second, (), 0, SLOTS)
    return jnp.where(jnp.arange(SLOTS) == chosen, SLOT_LEN, values).astype(jnp.int32)


def strengthened(drawn, stream_key, source, target, parts, factor):
    owner, partner = [(jnp.arange(drawn.shape[axis_at]) // (drawn.shape[axis_at] // parts)).reshape([-1 if axis == axis_at else 1 for axis in range(drawn.ndim)]) for axis_at in (source, target)]
    chosen = jax.random.permutation(stream_key, parts)[partner]
    strong = (owner == chosen) | (owner == (partner + parts // 2) % parts)
    return jnp.where(strong, factor * drawn, drawn)


def levels(key, shape, cuts, least, top_value):
    level, own = 1.0, jax.random.fold_in(key, 6)
    for dim, blocks in cuts:
        heights = jnp.exp(jax.random.uniform(jax.random.fold_in(own, dim), (blocks,), jnp.float32, least / len(cuts), top_value / len(cuts)))
        level = level * jnp.repeat(heights, shape[dim] // blocks).reshape([-1 if axis == dim else 1 for axis in range(len(shape))])
    return level


def gaussian(rng, dims, width, most, shards=(), kind=jnp.bfloat16):
    array = jax.random.normal(rng, dims, jnp.float32) * width
    if len(shards) > 0:
        array = levels(rng, dims, shards, -0.22, 0.18) * array
    return jnp.clip(array, min=-most, max=most).astype(kind)


def gaussian_with(own_key, dims, width, bound, cuts, heavy, held_as=jnp.bfloat16):
    values = width * jax.random.normal(own_key, dims, jnp.float32)
    if cuts:
        values = values * levels(own_key, dims, cuts, -0.22, 0.18)
    return jnp.clip(strengthened(values, jax.random.fold_in(own_key, 3), *heavy), -bound, bound).astype(held_as)


def setup_inputs(seed: int = 0) -> dict:
    key_list = jax.random.split(jax.random.key(seed), 16)
    tokens = gaussian_with(key_list[0], (TOKENS, D), 1.0, 6.0, ((0, 32),), (0, 1, 32, 2.75))
    cotangent = gaussian_with(key_list[1], (TOKENS, D), 1.0, 6.0, ((0, 32),), (0, 1, 32, 2.75))
    lengths = draw_lengths(jax.random.fold_in(key_list[15], 71), 0)
    norm_gain = jnp.clip(1.0 + 0.1 * jax.random.normal(key_list[3], (D,), jnp.float32), 0.5, 1.5).astype(jnp.bfloat16)
    norm_bias = gaussian(key_list[4], (D,), 0.3, 1.75, ((0, 8),))
    query_weight = gaussian(key_list[5], (D, D), D ** -0.5, 0.125, ((0, 8), (1, 4)))
    key_weight = gaussian(key_list[6], (D, D), D ** -0.5, 0.125, ((0, 8), (1, 4)))
    value_weight = gaussian(key_list[7], (D, D), D ** -0.5, 0.125, ((0, 8), (1, 4)))
    qkv_bias = gaussian(key_list[8], (3, HEADS, HEAD), 0.3, 1.75, ((1, 4), (2, 8)))
    proj_weight = gaussian(key_list[9], (D, D), 16 ** -0.5, 1.5, ((0, 4), (1, 8)))
    proj_bias = gaussian(key_list[10], (D,), 0.3, 1.75, ((0, 8),))
    up_weight = gaussian(key_list[11], (D, FF), D ** -0.5, 0.125, ((0, 8), (1, 4)))
    up_bias = gaussian(key_list[12], (FF // HEAD, HEAD), 0.5, 3.0, ((0, 4), (1, 8)))
    down_weight = gaussian(key_list[13], (FF, D), FF ** -0.5, 0.0625, ((0, 4), (1, 8)))
    down_bias = gaussian(key_list[14], (D,), 0.3, 1.75, ((0, 8),))
    return dict(tokens=tokens, cotangent=cotangent, lengths=lengths, norm_gain=norm_gain, norm_bias=norm_bias, query_weight=query_weight, key_weight=key_weight, value_weight=value_weight, qkv_bias=qkv_bias, proj_weight=proj_weight, proj_bias=proj_bias, up_weight=up_weight, up_bias=up_bias, down_weight=down_weight, down_bias=down_bias)


norm_eps = 1e-05
masked_score = -1000000000.0

@jax.custom_vjp
def low(v):
    return lax.optimization_barrier(v.astype(jnp.bfloat16)).astype(jnp.float32)

@jax.custom_vjp
def low_back(v):
    return v

def low_keep(v):
    return (low(v), None)

def low_pass(kept, grad):
    return (grad,)

def back_keep(v):
    return (v, None)

def back_low(kept, grad):
    return (low(grad),)
low.defvjp(low_keep, low_pass)
low_back.defvjp(back_keep, back_low)

def matmul(left, right):
    return jnp.dot(left, right, precision=lax.Precision.HIGHEST, preferred_element_type=jnp.float32)

def layer_norm(rows, gain, shift):
    center = rows - lax.optimization_barrier(jnp.mean(rows, axis=-1, keepdims=True))
    spread = lax.optimization_barrier(jnp.mean(center * center, axis=-1, keepdims=True))
    return center * lax.rsqrt(spread + norm_eps) * gain + shift

def rotary_tables(count, rot_dims):
    half = rot_dims // 2
    freq = 1.0 / 10000.0 ** (jnp.arange(half, dtype=jnp.float32) * (2.0 / rot_dims))
    angle = jnp.arange(count, dtype=jnp.float32)[:, None] * freq[None, :]
    return (jnp.cos(angle), jnp.sin(angle))

def rotary(field, cosine, sine):
    half = cosine.shape[1]
    first = field[..., :half]
    second = field[..., half:2 * half]
    cos_b = cosine[:, None, :]
    sin_b = sine[:, None, :]
    return jnp.concatenate([first * cos_b - second * sin_b, second * cos_b + first * sin_b, field[..., 2 * half:]], axis=-1)

def layer(rows, params, length):
    n_gain, n_shift, w_query, w_key, w_value, b_heads, w_proj, b_proj, w_up, b_up, w_down, b_down = params
    count = rows.shape[0]
    normed = low(layer_norm(rows, n_gain, n_shift))
    q_pre = low_back(matmul(normed, w_query) + b_heads[0].reshape(-1))
    k_pre = low_back(matmul(normed, w_key) + b_heads[1].reshape(-1))
    v_pre = low_back(matmul(normed, w_value) + b_heads[2].reshape(-1))
    cosine, sine = rotary_tables(count, ROT)
    q_rot = low(rotary(q_pre.reshape(count, HEADS, HEAD), cosine, sine))
    k_rot = low(rotary(k_pre.reshape(count, HEADS, HEAD), cosine, sine))
    v_low = low(v_pre).reshape(count, HEADS, HEAD)
    key_pos = jnp.arange(count)
    allowed = (key_pos[None, :] < length) & (key_pos[None, :] <= key_pos[:, None])
    scale = HEAD ** (-0.5)

    def one_head(item):
        q_head, k_head, v_head = item
        logits = matmul(q_head, k_head.T) * scale
        logits = low_back(jnp.where(allowed, logits, masked_score))
        probs = low(jax.nn.softmax(logits, axis=-1))
        return matmul(probs, v_head)
    mixed = lax.map(jax.checkpoint(one_head), (q_rot.transpose(1, 0, 2), k_rot.transpose(1, 0, 2), v_low.transpose(1, 0, 2)))
    mixed_low = low(low_back(mixed.transpose(1, 0, 2).reshape(count, HEADS * HEAD)))
    attn_out = matmul(mixed_low, w_proj) + b_proj
    up_pre = low_back(matmul(normed, w_up) + b_up.reshape(-1))
    act_low = low(jax.nn.gelu(up_pre, approximate=True))
    mlp_out = matmul(act_low, w_down) + b_down
    return rows + attn_out + mlp_out

def reference(tokens, cotangent, lengths, norm_gain, norm_bias, query_weight, key_weight, value_weight, qkv_bias, proj_weight, proj_bias, up_weight, up_bias, down_weight, down_bias):
    params = tuple((item.astype(jnp.float32) for item in (norm_gain, norm_bias, query_weight, key_weight, value_weight, qkv_bias, proj_weight, proj_bias, up_weight, up_bias, down_weight, down_bias)))
    slot_rows = tokens.astype(jnp.float32).reshape(SLOTS, SLOT_LEN, D)
    slot_grads = cotangent.astype(jnp.float32).reshape(SLOTS, SLOT_LEN, D)
    positions = jnp.arange(SLOT_LEN)

    def one_slot(total, item):
        rows, grad_rows, length = item
        result, back = jax.vjp(lambda r, p: layer(r, p, length), rows, params)
        live = (positions < length).astype(jnp.float32)[:, None]
        row_grad, param_grads = back(grad_rows * live)
        total = jax.tree.map(lambda a, b: a + b, total, param_grads)
        return (total, (result, row_grad))
    zero = jax.tree.map(jnp.zeros_like, params)
    total, (results, row_grads) = lax.scan(one_slot, zero, (slot_rows, slot_grads, lengths))
    output = results.reshape(TOKENS, D).astype(jnp.bfloat16)
    input_grad = row_grads.reshape(TOKENS, D)
    return (output, input_grad, total[0], total[1], total[2], total[3], total[4], total[5], total[6], total[7], total[8], total[9], total[10], total[11])
```

```python
import functools

import jax
import jax.numpy as jnp
from jax import lax
from jax.experimental import pallas as pl
from jax.experimental.pallas import tpu as pltpu
from jax.sharding import PartitionSpec as P

HEAD = 64
ROT = 32
LANES = 128
QBLOCK = 256
MLP_PARTS = (1, 1)
ATTN_RS = "line"
MLP_RS = ("sc", "line")

norm_eps = 1e-05
masked_score = -1000000000.0
F32 = jnp.float32
BF16 = jnp.bfloat16


def layer_norm(rows, gain, shift):
    center = rows - jnp.mean(rows, axis=-1, keepdims=True)
    spread = jnp.mean(center * center, axis=-1, keepdims=True)
    return center * lax.rsqrt(spread + norm_eps) * gain + shift


def product(left, right):
    return jnp.dot(left, right, preferred_element_type=F32)


def times_trans(left, right):
    return lax.dot_general(left, right, (((1,), (1,)), ((), ())), preferred_element_type=F32)


def inner_rows(left, right):
    return lax.dot_general(left, right, (((0,), (0,)), ((), ())), preferred_element_type=F32)


def rotary_lanes(count):
    half = ROT // 2
    lane = jnp.arange(LANES) % HEAD
    freq = 1.0 / 10000.0 ** ((lane % half).astype(F32) * (2.0 / ROT))
    angle = jnp.arange(count, dtype=F32)[:, None] * freq[None, :]
    cosine, sine = jnp.cos(angle), jnp.sin(angle)
    keep = jnp.where(lane < ROT, cosine, 1.0)
    from_left = jnp.where((lane >= half) & (lane < ROT), sine, 0.0)
    from_right = jnp.where(lane < half, -sine, 0.0)
    return keep, from_left, from_right


def turn(field, keep, from_left, from_right):
    half = ROT // 2
    left = pltpu.roll(field, half, 1)
    right = pltpu.roll(field, LANES - half, 1)
    return field * keep + left * from_left + right * from_right


def lane_iota(rows):
    return lax.broadcasted_iota(jnp.int32, (rows, LANES), 1)


def attn_fwd_kernel(len_ref, qkv_ref, keep_ref, left_ref, right_ref, q_ref, k_ref, v_ref, mix_ref, lse_ref):
    seq = qkv_ref.shape[0]
    scale = HEAD ** (-0.5)
    slot_len = len_ref[0]
    keep, left, right = keep_ref[...], left_ref[...], right_ref[...]
    q_low = turn(qkv_ref[:, :LANES], keep, left, right).astype(BF16) * jnp.asarray(scale, BF16)
    k_low = turn(qkv_ref[:, LANES : 2 * LANES], keep, left, right).astype(BF16)
    v_low = qkv_ref[:, 2 * LANES :].astype(BF16)
    q_ref[...] = q_low
    k_ref[...] = k_low
    v_ref[...] = v_low
    lane = lane_iota(seq)
    key_row = lax.broadcasted_iota(jnp.int32, (seq, LANES), 0)
    key_bias = jnp.where(key_row < slot_len, 0.0, masked_score).astype(BF16)
    one = jnp.ones((seq, LANES), BF16)
    none = jnp.zeros((seq, LANES), BF16)
    q_heads, k_heads, v_heads = [], [], []
    for head in range(2):
        inside = (lane // HEAD) == head
        flag = lane == (1 - head) * HEAD
        q_heads.append(jnp.where(inside, q_low, jnp.where(flag, one, none)))
        k_heads.append(jnp.where(flag, key_bias, k_low))
        v_heads.append(jnp.where(flag, one, v_low))
    rows = lax.broadcasted_iota(jnp.int32, (QBLOCK, QBLOCK), 0)
    cols = lax.broadcasted_iota(jnp.int32, (QBLOCK, QBLOCK), 1)
    causal = cols <= rows
    lane_q = lane_iota(QBLOCK)
    for block in range(seq // QBLOCK):
        start = block * QBLOCK
        mixed = []
        lses = []
        for head in range(2):
            q_block = q_heads[head][start : start + QBLOCK]
            diag = times_trans(q_block, k_heads[head][start : start + QBLOCK])
            diag = jnp.where(causal, diag, masked_score)
            top = jnp.max(diag, axis=1, keepdims=True)
            if block:
                past = times_trans(q_block, k_heads[head][:start])
                top = jnp.maximum(top, jnp.max(past, axis=1, keepdims=True))
            total = product(jnp.exp(diag - top).astype(BF16), v_heads[head][start : start + QBLOCK])
            if block:
                total += product(jnp.exp(past - top).astype(BF16), v_heads[head][:start])
            flag = (1 - head) * HEAD
            norm = total[:, flag : flag + 1]
            mixed.append(total * (1.0 / norm))
            lses.append(top + jnp.log(norm))
        mix_ref[start : start + QBLOCK, :] = jnp.where(lane_q < HEAD, mixed[0], mixed[1]).astype(BF16)
        lse_ref[start : start + QBLOCK, :] = jnp.where(lane_q < HEAD, lses[0], lses[1])


def attn_bwd_kernel(
    len_ref, q_ref, k_ref, v_ref, grad_ref, lse_ref, keep_ref, left_ref, right_ref, out_ref, dk_ref, dv_ref
):
    seq = q_ref.shape[0]
    scale = HEAD ** (-0.5)
    slot_len = len_ref[0]
    lane = lane_iota(seq)
    key_row = lax.broadcasted_iota(jnp.int32, (seq, LANES), 0)
    key_bias = jnp.where(key_row < slot_len, 0.0, masked_score).astype(BF16)
    none = jnp.zeros((seq, LANES), BF16)
    one = jnp.ones((seq, LANES), BF16)
    k_low = k_ref[...]
    v_low = v_ref[...]
    lane_q = lane_iota(QBLOCK)
    rows = lax.broadcasted_iota(jnp.int32, (QBLOCK, QBLOCK), 0)
    cols = lax.broadcasted_iota(jnp.int32, (QBLOCK, QBLOCK), 1)
    causal = cols <= rows
    k_heads, q_flags, q_clean, g_clean = [], [], [], []
    for head in range(2):
        inside = (lane // HEAD) == head
        flag = lane == (1 - head) * HEAD
        k_heads.append(jnp.where(flag, key_bias, k_low))
        clean = jnp.where(inside, q_ref[...], none)
        q_clean.append(clean)
        q_flags.append(jnp.where(flag, one, clean))
        g_clean.append(jnp.where(inside, grad_ref[...], none))
    blocks = seq // QBLOCK
    for block in range(blocks):
        start = block * QBLOCK
        stop = start + QBLOCK
        parts = []
        for head in range(2):
            lse = lse_ref[start:stop, head * HEAD : head * HEAD + 1]
            q_block = q_clean[head][start:stop]
            g_block = g_clean[head][start:stop]
            spans = [(start, stop)] + ([(0, start)] if block else [])
            kept = []
            row_dot = 0.0
            for low, high in spans:
                logits = times_trans(q_flags[head][start:stop], k_heads[head][low:high])
                if low == start:
                    logits = jnp.where(causal, logits, masked_score)
                probs = jnp.exp(logits - lse)
                prob_grad = times_trans(g_block, v_low[low:high])
                row_dot = row_dot + jnp.sum(probs * prob_grad, axis=1, keepdims=True)
                kept.append((low, high, probs, prob_grad))
            query = 0.0
            for low, high, probs, prob_grad in kept:
                score_grad = (probs * (prob_grad - row_dot)).astype(BF16)
                query = query + product(score_grad, k_low[low:high])
                key_part = inner_rows(score_grad, q_block)
                value_part = inner_rows(probs.astype(BF16), g_block)
                if low == start and head == 0:
                    dk_ref[low:high, :] = key_part
                    dv_ref[low:high, :] = value_part
                else:
                    dk_ref[low:high, :] += key_part
                    dv_ref[low:high, :] += value_part
            parts.append(query)
        query = jnp.where(lane_q < HEAD, parts[0], parts[1]) * scale
        out_ref[start:stop, :LANES] = turn(
            query, keep_ref[start:stop, :], -left_ref[start:stop, :], -right_ref[start:stop, :]
        ).astype(BF16)
    out_ref[:, LANES : 2 * LANES] = turn(
        dk_ref[...], keep_ref[...], -left_ref[...], -right_ref[...]
    ).astype(BF16)
    out_ref[:, 2 * LANES :] = dv_ref[...].astype(BF16)


def attention_forward(lengths, qkv, tables):
    seq, width = qkv.shape
    pairs = width // (3 * LANES)
    wide = pl.BlockSpec((seq, 3 * LANES), lambda p: (0, p))
    col = pl.BlockSpec((seq, LANES), lambda p: (0, p))
    whole = pl.BlockSpec((seq, LANES), lambda p: (0, 0))
    low = jax.ShapeDtypeStruct((seq, pairs * LANES), BF16)
    return pl.pallas_call(
        attn_fwd_kernel,
        grid=(pairs,),
        in_specs=[pl.BlockSpec(memory_space=pltpu.SMEM), wide, whole, whole, whole],
        out_specs=[col] * 5,
        out_shape=[low, low, low, low, jax.ShapeDtypeStruct((seq, pairs * LANES), F32)],
        compiler_params=pltpu.CompilerParams(
            dimension_semantics=("arbitrary",), vmem_limit_bytes=48 * 1024 * 1024
        ),
        cost_estimate=pl.CostEstimate(
            flops=pairs * 12 * seq * seq * LANES, bytes_accessed=pairs * seq * LANES * 24, transcendentals=0
        ),
        name="attn_fwd",
    )(lengths, qkv, *tables)


def attention_backward(lengths, q_low, k_low, v_low, mixed_grad, lse, tables):
    seq = q_low.shape[0]
    pairs = q_low.shape[1] // LANES
    wide = pl.BlockSpec((seq, 3 * LANES), lambda p: (0, p))
    col = pl.BlockSpec((seq, LANES), lambda p: (0, p))
    whole = pl.BlockSpec((seq, LANES), lambda p: (0, 0))
    return pl.pallas_call(
        attn_bwd_kernel,
        grid=(pairs,),
        in_specs=[pl.BlockSpec(memory_space=pltpu.SMEM)] + [col] * 5 + [whole] * 3,
        out_specs=wide,
        out_shape=jax.ShapeDtypeStruct((seq, pairs * 3 * LANES), BF16),
        scratch_shapes=[pltpu.VMEM((seq, LANES), F32), pltpu.VMEM((seq, LANES), F32)],
        compiler_params=pltpu.CompilerParams(
            dimension_semantics=("arbitrary",), vmem_limit_bytes=48 * 1024 * 1024
        ),
        cost_estimate=pl.CostEstimate(
            flops=pairs * 30 * seq * seq * LANES, bytes_accessed=pairs * seq * LANES * 24, transcendentals=0
        ),
        name="attn_bwd",
    )(lengths, q_low, k_low, v_low, mixed_grad, lse, *tables)


def swap_pairs(count, flip):
    return [(i, i ^ flip) for i in range(count)]


def line_scatter(grad, places):
    size = lax.axis_size("dp")
    stations = size // 2
    me = lax.axis_index("dp")
    core, place = me % 2, me // 2
    rows = grad.shape[0] // size
    stack = grad.reshape(stations, 2, rows, grad.shape[1])
    mine = lax.dynamic_index_in_dim(stack, core, 1, keepdims=False)
    other = lax.dynamic_index_in_dim(stack, 1 - core, 1, keepdims=False)
    got = lax.ppermute(other, "dp", swap_pairs(size, 1))
    pair = (mine.astype(F32) + got.astype(F32)).astype(BF16)

    def at(target):
        return lax.dynamic_index_in_dim(pair, jnp.clip(target, 0, stations - 1), 0, keepdims=False)

    up = down = None
    for step in range(1, stations):
        send_up = at(place + stations - step)
        send_down = at(place - stations + step)
        if step > 1:
            send_up = (send_up.astype(F32) + up.astype(F32)).astype(BF16)
            send_down = (send_down.astype(F32) + down.astype(F32)).astype(BF16)
        up_pairs = [(2 * z + c, 2 * z + 2 + c) for z in range(step) for c in range(2)]
        down_pairs = [(size - 1 - a, size - 1 - b) for a, b in up_pairs]
        up = lax.ppermute(send_up, "dp", up_pairs)
        down = lax.ppermute(send_down, "dp", down_pairs)
    return at(place).astype(F32) + up.astype(F32) + down.astype(F32)


def scatter(grad, how):
    if how == "line":
        return line_scatter(grad, None)
    return lax.psum_scatter(grad, "dp", scatter_dimension=0, tiled=True).astype(F32)


def gather_rows(parts, seq_rows):
    tensor = lax.axis_index("tensor")
    tok_rows, width = parts[0].shape
    whole = jnp.zeros((seq_rows, width), parts[0].dtype)
    for flip, part in enumerate(parts):
        whole = lax.dynamic_update_slice_in_dim(whole, part, (tensor ^ flip) * tok_rows, 0)
    return whole


def tensor_scatter(partial, tok_rows):
    count = lax.axis_size("tensor")
    tensor = lax.axis_index("tensor")

    def block(flip):
        return lax.dynamic_slice_in_dim(partial, (tensor ^ flip) * tok_rows, tok_rows, 0)

    total = block(0)
    low = partial.astype(BF16)
    for flip in range(1, count):
        sent = lax.dynamic_slice_in_dim(low, (tensor ^ flip) * tok_rows, tok_rows, 0)
        total = total + lax.ppermute(sent, "tensor", swap_pairs(count, flip)).astype(F32)
    return total


def on_device(
    tokens,
    cotangent,
    lengths,
    norm_gain,
    norm_bias,
    query_weight,
    key_weight,
    value_weight,
    qkv_bias,
    proj_weight,
    proj_bias,
    up_weight,
    up_bias,
    down_weight,
    down_bias,
):
    tensor_count = lax.axis_size("tensor")
    dp_count = lax.axis_size("dp")
    tensor = lax.axis_index("tensor")
    tok_rows, width = tokens.shape
    seq_rows = tok_rows * tensor_count
    heads_width = query_weight.shape[1]
    ff = up_weight.shape[1]
    pairs = heads_width // LANES
    slot_len = lengths[0]

    attn_in = jnp.concatenate(
        [
            item[:, p * LANES : (p + 1) * LANES]
            for p in range(pairs)
            for item in (query_weight, key_weight, value_weight)
        ],
        axis=1,
    )
    attn_pack = jnp.concatenate([attn_in, proj_weight.T], axis=1)
    attn_full = lax.all_gather(attn_pack, "dp", axis=0, tiled=True)
    down_t = down_weight.T
    weight_sum = sum(MLP_PARTS)
    edges = [0]
    for part in MLP_PARTS:
        edges.append(edges[-1] + ff * part // weight_sum)
    mlp_full = []
    for low, high in zip(edges[:-1], edges[1:]):
        pack = jnp.concatenate([up_weight[:, low:high], down_t[:, low:high]], axis=1)
        mlp_full.append(lax.all_gather(pack, "dp", axis=0, tiled=True))

    small = jnp.concatenate(
        [norm_gain, norm_bias, proj_bias, down_bias, qkv_bias.reshape(-1), up_bias.reshape(-1)]
    )
    small_all = lax.all_gather(small, "dp", axis=0, tiled=False)
    shard = norm_gain.shape[0]
    n_gain = small_all[:, :shard].reshape(-1).astype(F32)
    n_shift = small_all[:, shard : 2 * shard].reshape(-1).astype(F32)
    b_out = (
        small_all[:, 2 * shard : 3 * shard].astype(F32) + small_all[:, 3 * shard : 4 * shard].astype(F32)
    ).reshape(-1)
    heads_here = qkv_bias.shape[1]
    head_size = qkv_bias.size
    b_heads = (
        small_all[:, 4 * shard : 4 * shard + head_size]
        .reshape((dp_count,) + qkv_bias.shape)
        .transpose(1, 2, 0, 3)
        .reshape(3, pairs, LANES)
    )
    b_qkv = b_heads.transpose(1, 0, 2).reshape(-1).astype(F32)
    b_up = (
        small_all[:, 4 * shard + head_size :]
        .reshape((dp_count,) + up_bias.shape)
        .transpose(1, 0, 2)
        .reshape(-1)
        .astype(F32)
    )

    tok_parts = [tokens] + [
        lax.ppermute(tokens, "tensor", swap_pairs(tensor_count, flip)) for flip in range(1, tensor_count)
    ]
    grad_parts = [cotangent] + [
        lax.ppermute(cotangent, "tensor", swap_pairs(tensor_count, flip)) for flip in range(1, tensor_count)
    ]
    normed_parts = [layer_norm(part.astype(F32), n_gain, n_shift).astype(BF16) for part in tok_parts]
    normed = gather_rows(normed_parts, seq_rows)

    def masked(part, flip):
        pos = (tensor ^ flip) * tok_rows + jnp.arange(tok_rows)
        return jnp.where((pos < slot_len)[:, None], part, jnp.zeros_like(part))

    grad_all = gather_rows([masked(part, flip) for flip, part in enumerate(grad_parts)], seq_rows)

    tables = rotary_lanes(seq_rows)
    in_cols = 3 * heads_width
    w_qkv = attn_full[:, :in_cols]
    w_proj_t = attn_full[:, in_cols:]
    qkv = product(normed, w_qkv) + b_qkv
    q_low, k_low, v_low, mixed, lse = attention_forward(lengths, qkv, tables)
    mixed_grad = product(grad_all, w_proj_t).astype(BF16)
    proj_grad_t = inner_rows(grad_all, mixed).astype(BF16)
    qkv_grad = attention_backward(lengths, q_low, k_low, v_low, mixed_grad, lse, tables)
    in_grad = inner_rows(normed, qkv_grad).astype(BF16)
    attn_shard = scatter(jnp.concatenate([in_grad, proj_grad_t], axis=1), ATTN_RS)
    branch = times_trans(mixed, w_proj_t)
    normed_grad = times_trans(qkv_grad, w_qkv)
    head_bias_grad = jnp.sum(qkv_grad, axis=0, dtype=F32)

    mlp_shards = []
    up_bias_grads = []
    for index, (low, high) in enumerate(zip(edges[:-1], edges[1:])):
        units = high - low
        w_up = mlp_full[index][:, :units]
        w_down_t = mlp_full[index][:, units:]
        up_pre = product(normed, w_up) + b_up[low:high]
        act, gelu_back = jax.vjp(lambda value: jax.nn.gelu(value, approximate=True), up_pre)
        act = act.astype(BF16)
        up_pre_grad = gelu_back(product(grad_all, w_down_t))[0].astype(BF16)
        down_grad_t = inner_rows(grad_all, act).astype(BF16)
        up_grad = inner_rows(normed, up_pre_grad).astype(BF16)
        mlp_shards.append(scatter(jnp.concatenate([up_grad, down_grad_t], axis=1), MLP_RS[index]))
        up_bias_grads.append(jnp.sum(up_pre_grad, axis=0, dtype=F32))
        normed_grad = normed_grad + times_trans(up_pre_grad, w_up)
        branch = branch + times_trans(act, w_down_t)

    own = tokens.astype(F32)
    output = (own + tensor_scatter(branch, tok_rows) + b_out).astype(BF16)
    own_normed_grad = tensor_scatter(normed_grad, tok_rows)
    _, norm_back = jax.vjp(layer_norm, own, n_gain, n_shift)
    input_part, gain_part, shift_part = norm_back(own_normed_grad)
    input_grad = masked(cotangent, 0).astype(F32) + input_part
    gain_sum, shift_sum = lax.psum((gain_part, shift_part), "tensor")

    head_part = (
        head_bias_grad.reshape(pairs, 3, LANES)
        .transpose(1, 0, 2)
        .reshape(3, heads_here, dp_count, HEAD // dp_count)
        .transpose(2, 0, 1, 3)
        .reshape(dp_count, -1)
    )
    up_part = (
        jnp.concatenate(up_bias_grads)
        .reshape(up_bias.shape[0], dp_count, -1)
        .transpose(1, 0, 2)
        .reshape(dp_count, -1)
    )
    out_bias_part = jnp.sum(grad_all, axis=0, dtype=F32).reshape(dp_count, shard)
    small_grad = jnp.concatenate(
        [gain_sum.reshape(dp_count, shard), shift_sum.reshape(dp_count, shard), out_bias_part, head_part, up_part],
        axis=1,
    ).astype(BF16)
    small_out = lax.psum_scatter(small_grad, "dp", scatter_dimension=0, tiled=True)[0].astype(F32)
    gain_grad = small_out[:shard]
    shift_grad = small_out[shard : 2 * shard]
    out_bias = small_out[2 * shard : 3 * shard]
    head_out = small_out[3 * shard : 3 * shard + head_size].reshape(qkv_bias.shape)
    up_bias_out = small_out[3 * shard + head_size :].reshape(up_bias.shape)

    def part_of(which):
        return jnp.concatenate(
            [attn_shard[:, (3 * p + which) * LANES : (3 * p + which + 1) * LANES] for p in range(pairs)], axis=1
        )

    up_out = jnp.concatenate([item[:, : item.shape[1] // 2] for item in mlp_shards], axis=1)
    down_out = jnp.concatenate([item[:, item.shape[1] // 2 :].T for item in mlp_shards], axis=0)
    return (
        output,
        input_grad,
        gain_grad,
        shift_grad,
        part_of(0),
        part_of(1),
        part_of(2),
        head_out,
        attn_shard[:, in_cols:].T,
        out_bias,
        up_out,
        up_bias_out,
        down_out,
        out_bias,
    )


def solution(mesh):
    rows = P(("dp", "tensor"), None)
    both = P("dp", "tensor")
    turned = P("tensor", "dp")
    heads = P(None, "tensor", "dp")
    vec = P("dp")
    return jax.shard_map(
        on_device,
        mesh=mesh,
        in_specs=(rows, rows, vec, vec, vec, both, both, both, heads, turned, vec, both, turned, turned, vec),
        out_specs=(rows, rows, vec, vec, both, both, both, heads, turned, vec, both, turned, turned, vec),
        check_vma=False,
    )
```

```python
import functools

import jax
import jax.numpy as jnp
from jax import lax
from jax.experimental import pallas as pl
from jax.experimental.pallas import tpu as pltpu
from jax.sharding import PartitionSpec as P

HEAD = 64
ROT = 32
LANES = 128
QBLOCK = 256
MLP_PARTS = (9, 7)

norm_eps = 1e-05
masked_score = -1000000000.0
F32 = jnp.float32
BF16 = jnp.bfloat16


def layer_norm(rows, gain, shift):
    center = rows - jnp.mean(rows, axis=-1, keepdims=True)
    spread = jnp.mean(center * center, axis=-1, keepdims=True)
    return center * lax.rsqrt(spread + norm_eps) * gain + shift


def product(left, right):
    return jnp.dot(left, right, preferred_element_type=F32)


def times_trans(left, right):
    return lax.dot_general(left, right, (((1,), (1,)), ((), ())), preferred_element_type=F32)


def inner_rows(left, right):
    return lax.dot_general(left, right, (((0,), (0,)), ((), ())), preferred_element_type=F32)


def rotary_lanes(count):
    half = ROT // 2
    lane = jnp.arange(LANES) % HEAD
    freq = 1.0 / 10000.0 ** ((lane % half).astype(F32) * (2.0 / ROT))
    angle = jnp.arange(count, dtype=F32)[:, None] * freq[None, :]
    cosine, sine = jnp.cos(angle), jnp.sin(angle)
    keep = jnp.where(lane < ROT, cosine, 1.0)
    from_left = jnp.where((lane >= half) & (lane < ROT), sine, 0.0)
    from_right = jnp.where(lane < half, -sine, 0.0)
    return keep, from_left, from_right


def turn(field, keep, from_left, from_right):
    half = ROT // 2
    left = pltpu.roll(field, half, 1)
    right = pltpu.roll(field, LANES - half, 1)
    return field * keep + left * from_left + right * from_right


def lane_iota(rows):
    return lax.broadcasted_iota(jnp.int32, (rows, LANES), 1)


def attn_fwd_kernel(len_ref, qkv_ref, keep_ref, left_ref, right_ref, q_ref, k_ref, v_ref, mix_ref, lse_ref):
    seq = qkv_ref.shape[0]
    scale = HEAD ** (-0.5)
    slot_len = len_ref[0]
    keep, left, right = keep_ref[...], left_ref[...], right_ref[...]
    q_low = turn(qkv_ref[:, :LANES], keep, left, right).astype(BF16) * jnp.asarray(scale, BF16)
    k_low = turn(qkv_ref[:, LANES : 2 * LANES], keep, left, right).astype(BF16)
    v_low = qkv_ref[:, 2 * LANES :].astype(BF16)
    q_ref[...] = q_low
    k_ref[...] = k_low
    v_ref[...] = v_low
    lane = lane_iota(seq)
    key_row = lax.broadcasted_iota(jnp.int32, (seq, LANES), 0)
    key_bias = jnp.where(key_row < slot_len, 0.0, masked_score).astype(BF16)
    one = jnp.ones((seq, LANES), BF16)
    none = jnp.zeros((seq, LANES), BF16)
    q_heads, k_heads, v_heads = [], [], []
    for head in range(2):
        inside = (lane // HEAD) == head
        flag = lane == (1 - head) * HEAD
        q_heads.append(jnp.where(inside, q_low, jnp.where(flag, one, none)))
        k_heads.append(jnp.where(flag, key_bias, k_low))
        v_heads.append(jnp.where(flag, one, v_low))
    rows = lax.broadcasted_iota(jnp.int32, (QBLOCK, QBLOCK), 0)
    cols = lax.broadcasted_iota(jnp.int32, (QBLOCK, QBLOCK), 1)
    causal = cols <= rows
    lane_q = lane_iota(QBLOCK)
    for block in range(seq // QBLOCK):
        start = block * QBLOCK
        mixed = []
        lses = []
        for head in range(2):
            q_block = q_heads[head][start : start + QBLOCK]
            diag = times_trans(q_block, k_heads[head][start : start + QBLOCK])
            diag = jnp.where(causal, diag, masked_score)
            top = jnp.max(diag, axis=1, keepdims=True)
            if block:
                past = times_trans(q_block, k_heads[head][:start])
                top = jnp.maximum(top, jnp.max(past, axis=1, keepdims=True))
            total = product(jnp.exp(diag - top).astype(BF16), v_heads[head][start : start + QBLOCK])
            if block:
                total += product(jnp.exp(past - top).astype(BF16), v_heads[head][:start])
            flag = (1 - head) * HEAD
            norm = total[:, flag : flag + 1]
            mixed.append(total * (1.0 / norm))
            lses.append(top + jnp.log(norm))
        mix_ref[start : start + QBLOCK, :] = jnp.where(lane_q < HEAD, mixed[0], mixed[1]).astype(BF16)
        lse_ref[start : start + QBLOCK, :] = jnp.where(lane_q < HEAD, lses[0], lses[1])


def attn_bwd_kernel(
    len_ref, q_ref, k_ref, v_ref, grad_ref, lse_ref, keep_ref, left_ref, right_ref, out_ref, dk_ref, dv_ref
):
    seq = q_ref.shape[0]
    scale = HEAD ** (-0.5)
    slot_len = len_ref[0]
    lane = lane_iota(seq)
    key_row = lax.broadcasted_iota(jnp.int32, (seq, LANES), 0)
    key_bias = jnp.where(key_row < slot_len, 0.0, masked_score).astype(BF16)
    none = jnp.zeros((seq, LANES), BF16)
    one = jnp.ones((seq, LANES), BF16)
    k_low = k_ref[...]
    v_low = v_ref[...]
    lane_q = lane_iota(QBLOCK)
    rows = lax.broadcasted_iota(jnp.int32, (QBLOCK, QBLOCK), 0)
    cols = lax.broadcasted_iota(jnp.int32, (QBLOCK, QBLOCK), 1)
    causal = cols <= rows
    k_heads, q_flags, q_clean, g_clean = [], [], [], []
    for head in range(2):
        inside = (lane // HEAD) == head
        flag = lane == (1 - head) * HEAD
        k_heads.append(jnp.where(flag, key_bias, k_low))
        clean = jnp.where(inside, q_ref[...], none)
        q_clean.append(clean)
        q_flags.append(jnp.where(flag, one, clean))
        g_clean.append(jnp.where(inside, grad_ref[...], none))
    blocks = seq // QBLOCK
    for block in range(blocks):
        start = block * QBLOCK
        stop = start + QBLOCK
        parts = []
        for head in range(2):
            lse = lse_ref[start:stop, head * HEAD : head * HEAD + 1]
            q_block = q_clean[head][start:stop]
            g_block = g_clean[head][start:stop]
            spans = [(start, stop)] + ([(0, start)] if block else [])
            kept = []
            row_dot = 0.0
            for low, high in spans:
                logits = times_trans(q_flags[head][start:stop], k_heads[head][low:high])
                if low == start:
                    logits = jnp.where(causal, logits, masked_score)
                probs = jnp.exp(logits - lse)
                prob_grad = times_trans(g_block, v_low[low:high])
                row_dot = row_dot + jnp.sum(probs * prob_grad, axis=1, keepdims=True)
                kept.append((low, high, probs, prob_grad))
            query = 0.0
            for low, high, probs, prob_grad in kept:
                score_grad = (probs * (prob_grad - row_dot)).astype(BF16)
                query = query + product(score_grad, k_low[low:high])
                key_part = inner_rows(score_grad, q_block)
                value_part = inner_rows(probs.astype(BF16), g_block)
                if low == start and head == 0:
                    dk_ref[low:high, :] = key_part
                    dv_ref[low:high, :] = value_part
                else:
                    dk_ref[low:high, :] += key_part
                    dv_ref[low:high, :] += value_part
            parts.append(query)
        query = jnp.where(lane_q < HEAD, parts[0], parts[1]) * scale
        out_ref[start:stop, :LANES] = turn(
            query, keep_ref[start:stop, :], -left_ref[start:stop, :], -right_ref[start:stop, :]
        ).astype(BF16)
    out_ref[:, LANES : 2 * LANES] = turn(
        dk_ref[...], keep_ref[...], -left_ref[...], -right_ref[...]
    ).astype(BF16)
    out_ref[:, 2 * LANES :] = dv_ref[...].astype(BF16)


def attention_forward(lengths, qkv, tables):
    seq, width = qkv.shape
    pairs = width // (3 * LANES)
    wide = pl.BlockSpec((seq, 3 * LANES), lambda p: (0, p))
    col = pl.BlockSpec((seq, LANES), lambda p: (0, p))
    whole = pl.BlockSpec((seq, LANES), lambda p: (0, 0))
    low = jax.ShapeDtypeStruct((seq, pairs * LANES), BF16)
    return pl.pallas_call(
        attn_fwd_kernel,
        grid=(pairs,),
        in_specs=[pl.BlockSpec(memory_space=pltpu.SMEM), wide, whole, whole, whole],
        out_specs=[col] * 5,
        out_shape=[low, low, low, low, jax.ShapeDtypeStruct((seq, pairs * LANES), F32)],
        compiler_params=pltpu.CompilerParams(
            dimension_semantics=("arbitrary",), vmem_limit_bytes=48 * 1024 * 1024
        ),
        cost_estimate=pl.CostEstimate(
            flops=pairs * 12 * seq * seq * LANES, bytes_accessed=pairs * seq * LANES * 24, transcendentals=0
        ),
        name="attn_fwd",
    )(lengths, qkv, *tables)


def attention_backward(lengths, q_low, k_low, v_low, mixed_grad, lse, tables):
    seq = q_low.shape[0]
    pairs = q_low.shape[1] // LANES
    wide = pl.BlockSpec((seq, 3 * LANES), lambda p: (0, p))
    col = pl.BlockSpec((seq, LANES), lambda p: (0, p))
    whole = pl.BlockSpec((seq, LANES), lambda p: (0, 0))
    return pl.pallas_call(
        attn_bwd_kernel,
        grid=(pairs,),
        in_specs=[pl.BlockSpec(memory_space=pltpu.SMEM)] + [col] * 5 + [whole] * 3,
        out_specs=wide,
        out_shape=jax.ShapeDtypeStruct((seq, pairs * 3 * LANES), BF16),
        scratch_shapes=[pltpu.VMEM((seq, LANES), F32), pltpu.VMEM((seq, LANES), F32)],
        compiler_params=pltpu.CompilerParams(
            dimension_semantics=("arbitrary",), vmem_limit_bytes=48 * 1024 * 1024
        ),
        cost_estimate=pl.CostEstimate(
            flops=pairs * 30 * seq * seq * LANES, bytes_accessed=pairs * seq * LANES * 24, transcendentals=0
        ),
        name="attn_bwd",
    )(lengths, q_low, k_low, v_low, mixed_grad, lse, *tables)


def swap_pairs(count, flip):
    return [(i, i ^ flip) for i in range(count)]


def bits_below(count):
    return [1 << b for b in range(count.bit_length() - 1)]


def norm_rows(rows):
    center = rows - jnp.mean(rows, axis=-1, keepdims=True)
    spread = jnp.mean(center * center, axis=-1, keepdims=True)
    return center * lax.rsqrt(spread + norm_eps)


def joined(pieces, low, high):
    return jnp.concatenate([piece[low:high, :].astype(F32) for piece in pieces], axis=1)


def norm_kernel(at_ref, *refs):
    *pieces, gain_ref, shift_ref = refs[:-2]
    out_ref = refs[-1]
    rows = out_ref.shape[0]
    for low in range(0, rows, 32):
        part = norm_rows(joined(pieces, low, low + 32))
        out_ref[low : low + 32, :] = (part * gain_ref[...] + shift_ref[...]).astype(BF16)


def mask_kernel(at_ref, len_ref, *refs):
    pieces = refs[:-2]
    out_ref = refs[-1]
    rows, width = out_ref.shape
    pos = at_ref[0] * rows + lax.broadcasted_iota(jnp.int32, (rows, width), 0)
    whole = jnp.concatenate([piece[...] for piece in pieces], axis=1)
    out_ref[...] = jnp.where(pos < len_ref[0], whole, jnp.zeros_like(whole))


def place_rows(kernel, name, seq_rows, pieces, extra, scalars, buffer):
    tok_rows = pieces[0].shape[0]
    width = sum(piece.shape[1] for piece in pieces)
    count = len(scalars)
    whole = lambda item: pl.BlockSpec(item.shape, lambda i, *s: (0, 0))
    last = [] if buffer is None else [buffer]
    operands = list(pieces) + list(extra) + (last or [extra[0] if extra else pieces[0]])
    specs = [whole(item) for item in list(pieces) + list(extra)] + [pl.BlockSpec(memory_space=pl.ANY)]
    return pl.pallas_call(
        kernel,
        grid_spec=pltpu.PrefetchScalarGridSpec(
            num_scalar_prefetch=count,
            grid=(1,),
            in_specs=specs,
            out_specs=pl.BlockSpec((tok_rows, width), lambda i, at, *s: (at[0], 0)),
        ),
        out_shape=jax.ShapeDtypeStruct((seq_rows, width), BF16),
        input_output_aliases={count + len(operands) - 1: 0} if last else {},
        name=name,
    )(*scalars, *operands)


def sums_kernel(counts, at_ref, *refs):
    parts, (grad_ref, out_ref, gain_acc, shift_acc) = list(refs[:-4]), refs[-4:]
    rows = parts[0].shape[0]
    gain_acc[...] = jnp.zeros_like(gain_acc)
    shift_acc[...] = jnp.zeros_like(shift_acc)
    step = gain_acc.shape[0]
    for flip, count in enumerate(counts):
        pieces = [parts.pop(0) for _ in range(count)]
        base = pl.multiple_of((at_ref[0] ^ flip) * rows, rows)
        for low in range(0, rows, step):
            grad = grad_ref[pl.ds(base + low, step), :].astype(F32)
            gain_acc[...] += grad * norm_rows(joined(pieces, low, low + step))
            shift_acc[...] += grad
    out_ref[0:1, :] = jnp.sum(gain_acc[...], axis=0, keepdims=True)
    out_ref[1:2, :] = jnp.sum(shift_acc[...], axis=0, keepdims=True)


def norm_sums(tensor, parts, grad):
    width = grad.shape[1]
    pieces = [piece for part in parts for piece in part]
    vmem = pl.BlockSpec(memory_space=pltpu.VMEM)
    return pl.pallas_call(
        functools.partial(sums_kernel, [len(part) for part in parts]),
        in_specs=[pl.BlockSpec(memory_space=pltpu.SMEM)] + [vmem] * (len(pieces) + 1),
        out_specs=vmem,
        out_shape=jax.ShapeDtypeStruct((2, width), F32),
        scratch_shapes=[pltpu.VMEM((32, width), F32), pltpu.VMEM((32, width), F32)],
        compiler_params=pltpu.CompilerParams(vmem_limit_bytes=32 * 1024 * 1024),
        cost_estimate=pl.CostEstimate(flops=16 * grad.size, bytes_accessed=4 * grad.size, transcendentals=0),
        name="norm_sums",
    )(tensor, *pieces, grad)


def weight_kernel(at_ref, left_a, right_a, left_b, right_b, out_ref):
    width = right_a.shape[1]
    out_ref[:, :width] = inner_rows(left_a[...], right_a[...]).astype(BF16)
    out_ref[:, width:] = inner_rows(left_b[...], right_b[...]).astype(BF16)


def weight_grads(left_a, right_a, left_b, right_b, first, stride, blocks, rows):
    seq = left_a.shape[0]
    width = right_a.shape[1] + right_b.shape[1]
    block = pl.BlockSpec((seq, rows), lambda i, at: (0, stride * i + at[0]))
    whole = lambda item: pl.BlockSpec(item.shape, lambda i, at: (0, 0))
    return pl.pallas_call(
        weight_kernel,
        grid_spec=pltpu.PrefetchScalarGridSpec(
            num_scalar_prefetch=1,
            grid=(blocks,),
            in_specs=[block, whole(right_a), block, whole(right_b)],
            out_specs=pl.BlockSpec((rows, width), lambda i, at: (i, 0)),
        ),
        out_shape=jax.ShapeDtypeStruct((blocks * rows, width), BF16),
        compiler_params=pltpu.CompilerParams(vmem_limit_bytes=32 * 1024 * 1024),
        cost_estimate=pl.CostEstimate(
            flops=2 * seq * blocks * rows * width,
            bytes_accessed=2 * seq * (width + 2 * blocks * rows) + 2 * blocks * rows * width,
            transcendentals=0,
        ),
        name="weight_grads",
    )(first, left_a, right_a, left_b, right_b)


def tie(*values):
    return lax.optimization_barrier(values)


class LineScatter:
    def __init__(self, left_a, right_a, left_b, right_b):
        self.size = lax.axis_size("dp")
        self.stations = self.size // 2
        me = lax.axis_index("dp")
        self.core, self.place = me % 2, me // 2
        self.rows = left_a.shape[1] // self.size
        self.other = weight_grads(
            left_a, right_a, left_b, right_b, (1 - self.core)[None], 2, self.stations, self.rows
        )
        self.step = 0

    def finish_pair(self, left_a, right_a, left_b, right_b):
        self.mine = weight_grads(
            left_a, right_a, left_b, right_b, self.core[None], 2, self.stations, self.rows
        )
        self.held = (lax.ppermute(self.other, "dp", swap_pairs(self.size, 1)),)

    def at(self, target):
        target = jnp.clip(target, 0, self.stations - 1)
        pick = lambda item: lax.dynamic_slice_in_dim(item, target * self.rows, self.rows, 0).astype(F32)
        return pick(self.mine) + pick(self.got)

    def next_sends(self):
        if self.step == 0:
            (self.got,) = self.held
            self.held = (None, None)
        self.step += 1
        if self.step >= self.stations:
            up, down = self.held
            self.total = self.at(self.place) + up.astype(F32) + down.astype(F32)
            return ()
        up, down = self.held if len(self.held) == 2 else self.held * 2
        above = self.place + self.stations - self.step
        below = self.place - self.stations + self.step
        add = lambda sent, item: (sent if item is None else sent + item.astype(F32)).astype(BF16)
        if 2 * self.step < self.stations - 1:
            near = 2 * self.place < self.stations
            sent = self.at(jnp.where(near, above, below))
            return (add(sent, up),)
        return add(self.at(above), up), add(self.at(below), down)

    def send(self, sends):
        to_up = [(2 * z + c, 2 * z + 2 + c) for z in range(self.step) for c in range(2)]
        to_down = [(self.size - 1 - a, self.size - 1 - b) for a, b in to_up]
        if len(sends) == 1:
            self.held = (lax.ppermute(sends[0], "dp", to_up + to_down),)
        else:
            self.held = tuple(lax.ppermute(item, "dp", way) for item, way in zip(sends, (to_up, to_down)))

    def done(self):
        return self.step >= self.stations


def weave_kernel(at_ref, mine_ref, got_ref, out_ref):
    same = pl.program_id(0) % 2 == at_ref[1]

    @pl.when(same)
    def _():
        out_ref[...] = mine_ref[...]

    @pl.when(jnp.logical_not(same))
    def _():
        out_ref[...] = got_ref[...]


class LineGather:
    def __init__(self, pack):
        self.size = lax.axis_size("dp")
        self.stations = self.size // 2
        me = lax.axis_index("dp")
        self.core, self.place = me % 2, me // 2
        self.pack = pack
        self.step = 1
        self.came = []
        self.send((pack, pack))

    def send(self, sends):
        if self.step == self.stations:
            self.held = (lax.ppermute(sends[0], "dp", swap_pairs(self.size, 1)),)
            return
        to_up = [(2 * z + c, 2 * z + 2 + c) for z in range(self.step - 1, self.stations - 1) for c in range(2)]
        to_down = [(self.size - 1 - a, self.size - 1 - b) for a, b in to_up]
        if len(sends) == 1:
            self.held = (lax.ppermute(sends[0], "dp", to_up + to_down),)
        else:
            self.held = tuple(lax.ppermute(item, "dp", way) for item, way in zip(sends, (to_up, to_down)))

    def next_sends(self):
        self.step += 1
        if self.step == self.stations + 1:
            self.full = self.weave(self.stack, self.held[0])
            return ()
        up, down = self.held if len(self.held) == 2 else self.held * 2
        self.came.append((up, down))
        if self.step == self.stations:
            parts = [self.pack]
            for far in range(1, self.stations):
                ahead = self.place + far < self.stations
                parts.append(jnp.where(ahead, self.came[far - 1][1], self.came[self.stations - far - 1][0]))
            self.stack = jnp.concatenate(parts)
            return (self.stack,)
        if 2 * self.step > self.stations + 1:
            return (jnp.where(2 * self.place >= self.stations, up, down),)
        return up, down

    def weave(self, mine, got):
        rows, width = self.pack.shape
        stations = self.stations
        half = pl.BlockSpec((rows, width), lambda i, at: ((i // 2 + stations - at[0]) % stations, 0))
        return pl.pallas_call(
            weave_kernel,
            grid_spec=pltpu.PrefetchScalarGridSpec(
                num_scalar_prefetch=1,
                grid=(self.size,),
                in_specs=[half, half],
                out_specs=pl.BlockSpec((rows, width), lambda i, at: (i, 0)),
            ),
            out_shape=jax.ShapeDtypeStruct((self.size * rows, width), BF16),
            cost_estimate=pl.CostEstimate(
                flops=0, bytes_accessed=6 * self.size * rows * width, transcendentals=0
            ),
            name="weave",
        )(jnp.stack([self.place, self.core]).astype(jnp.int32), mine, got)

    def done(self):
        return self.step > self.stations


def advance(lines, *values):
    lines = [line for line in lines if not line.done()]
    flat = tie(*[item for line in lines for item in line.held], *values)
    for line in lines:
        line.held, flat = flat[: len(line.held)], flat[len(line.held) :]
    sends = [line.next_sends() for line in lines]
    flat = tie(*[item for sent in sends for item in sent], *flat)
    for line, sent in zip(lines, sends):
        if sent:
            line.send(flat[: len(sent)])
            flat = flat[len(sent) :]
    return flat


def natural_grads(left_a, right_a, left_b, right_b):
    size = lax.axis_size("dp")
    zero = jnp.zeros((1,), jnp.int32)
    return weight_grads(left_a, right_a, left_b, right_b, zero, 1, size, left_a.shape[1] // size)


class TensorScatter:
    def __init__(self, partial, tok_rows):
        self.count = lax.axis_size("tensor")
        tensor = lax.axis_index("tensor")
        half = partial.shape[1] // 2

        def block(flip, side):
            start = ((tensor ^ flip) * tok_rows, side * half)
            return lax.dynamic_slice(partial, start, (tok_rows, half))

        self.block, self.tok_rows = block, tok_rows
        self.rest = []
        if self.count > 4:
            self.rest = [
                lax.ppermute(block(flip, side), "tensor", swap_pairs(self.count, flip))
                for side in (0, 1)
                for flip in range(1, self.count)
            ]
            return
        self.first = []
        for side, flip in ((0, 1), (1, 2)):
            sent = jnp.concatenate([block(flip, side), block(3, side)])
            self.first.append(lax.ppermute(sent, "tensor", swap_pairs(self.count, flip)))

    def second(self, *values):
        if self.count > 4:
            return values
        self.total = []
        flat = tie(*self.first, *values)
        self.first, values = flat[:2], flat[2:]
        for side, flip in ((0, 1), (1, 2)):
            got = self.first[side].astype(F32)
            far = (self.block(3 - flip, side).astype(F32) + got[self.tok_rows :]).astype(BF16)
            near = self.block(0, side).astype(F32) + got[: self.tok_rows]
            self.total.append((near, lax.ppermute(far, "tensor", swap_pairs(self.count, 3 - flip))))
        return values

    def result(self, *values):
        if self.count > 4:
            flat = tie(*self.rest, *values)
            many = self.count - 1
            total = [
                sum((item.astype(F32) for item in flat[side * many : (side + 1) * many]), self.block(0, side).astype(F32))
                for side in (0, 1)
            ]
            return (jnp.concatenate(total, axis=1),) + flat[2 * many :]
        flat = tie(*[item for _, item in self.total], *values)
        total = [near + item.astype(F32) for (near, _), item in zip(self.total, flat)]
        return (jnp.concatenate(total, axis=1),) + flat[2:]


def all_sum(value, axis):
    count = lax.axis_size(axis)
    for bit in bits_below(count):
        value = value + lax.ppermute(value, axis, swap_pairs(count, bit))
    return value


def gelu_pair(value):
    slope = (2.0 / jnp.pi) ** 0.5
    square = value * value
    flat = jnp.tanh(slope * value * (1.0 + 0.044715 * square))
    act = 0.5 * value * (1.0 + flat)
    back = 0.5 * (1.0 + flat) + 0.5 * value * (1.0 - flat * flat) * slope * (1.0 + 3 * 0.044715 * square)
    return act.astype(BF16), back.astype(BF16)


def on_device(
    tokens,
    cotangent,
    lengths,
    norm_gain,
    norm_bias,
    query_weight,
    key_weight,
    value_weight,
    qkv_bias,
    proj_weight,
    proj_bias,
    up_weight,
    up_bias,
    down_weight,
    down_bias,
):
    tensor_count = lax.axis_size("tensor")
    dp_count = lax.axis_size("dp")
    tensor = lax.axis_index("tensor")
    place = lax.axis_index("dp")
    tok_rows, width = tokens.shape
    seq_rows = tok_rows * tensor_count
    heads_width = query_weight.shape[1]
    ff = up_weight.shape[1]
    pairs = heads_width // LANES
    slot_len = lengths[0]

    small = jnp.concatenate(
        [norm_gain, norm_bias, proj_bias, down_bias, qkv_bias.reshape(-1), up_bias.reshape(-1)]
    )
    mine_row = (jnp.arange(dp_count) == place)[:, None]
    small_all = all_sum(jnp.where(mine_row, small[None, :], jnp.zeros((), BF16)), "dp")
    shard = norm_gain.shape[0]
    b_out = (
        small_all[:, 2 * shard : 3 * shard].astype(F32) + small_all[:, 3 * shard : 4 * shard].astype(F32)
    ).reshape(-1)
    heads_here = qkv_bias.shape[1]
    head_size = qkv_bias.size
    b_heads = (
        small_all[:, 4 * shard : 4 * shard + head_size]
        .reshape((dp_count,) + qkv_bias.shape)
        .transpose(1, 2, 0, 3)
        .reshape(3, pairs, LANES)
    )
    b_qkv = b_heads.transpose(1, 0, 2).reshape(-1).astype(F32)
    b_up = (
        small_all[:, 4 * shard + head_size :]
        .reshape((dp_count,) + up_bias.shape)
        .transpose(1, 0, 2)
        .reshape(-1)
        .astype(F32)
    )

    down_t = down_weight.T
    weight_sum = sum(MLP_PARTS)
    edges = [0]
    for part in MLP_PARTS:
        edges.append(edges[-1] + ff * part // weight_sum)

    def mlp_pack(index):
        low, high = edges[index], edges[index + 1]
        return jnp.concatenate([up_weight[:, low:high], down_t[:, low:high]], axis=1)

    attn_in = [
        item[:, p * LANES : (p + 1) * LANES]
        for p in range(pairs)
        for item in (query_weight, key_weight, value_weight)
    ]
    attn_pack = jnp.concatenate(attn_in + [proj_weight.T], axis=1)
    attn_full = lax.all_gather(attn_pack, "dp", axis=0, tiled=True)
    near_pack, far_pack = mlp_pack(0), mlp_pack(1)

    half = width // 2

    def direct(rows, flip):
        return lax.ppermute(rows, "tensor", swap_pairs(tensor_count, flip))

    def third(first, second):
        return [direct(first[:, :half], 2), direct(second[:, half:], 1)]

    tok_one, tok_two, small_all = tie(direct(tokens, 1), direct(tokens, 2), small_all)
    tok_one, near_pack = tie(tok_one, near_pack)
    near_full = lax.all_gather(near_pack, "dp", axis=0, tiled=True)
    tok_three = third(tok_one, tok_two)
    cot_held, tok_one, tok_two = tie(cotangent, tok_one, tok_two)
    cot_one, cot_two = direct(cot_held, 1), direct(cot_held, 2)
    more = range(4, tensor_count)
    tok_more = [[direct(tokens, flip)] for flip in more]

    n_gain = small_all[:, :shard].reshape(-1).astype(F32)
    n_shift = small_all[:, shard : 2 * shard].reshape(-1).astype(F32)

    def where_of(flip):
        return (tensor ^ flip).astype(jnp.int32)[None]

    gain_row, shift_row = n_gain[None, :], n_shift[None, :]
    tok_parts = [[tokens], [tok_one], [tok_two], tok_three] + tok_more
    normed = None
    for flip in range(tensor_count):
        if flip == 3:
            normed, cot_one, cot_two = tie(normed, cot_one, cot_two)
            cot_three = third(cot_one, cot_two)
        normed = place_rows(
            norm_kernel, "norm_rows", seq_rows, tok_parts[flip], [gain_row, shift_row], [where_of(flip)], normed
        )
    cot_parts = [[cotangent], [cot_one], [cot_two], cot_three] + [[direct(cot_held, flip)] for flip in more]
    grad_all = None
    for flip in range(tensor_count):
        grad_all = place_rows(
            mask_kernel, "mask_rows", seq_rows, cot_parts[flip], [], [where_of(flip), lengths], grad_all
        )
    normed, grad_all, far_pack = tie(normed, grad_all, far_pack)

    tables = rotary_lanes(seq_rows)
    in_cols = 3 * heads_width
    w_qkv = attn_full[:, :in_cols]
    w_proj_t = attn_full[:, in_cols:]
    qkv = product(normed, w_qkv) + b_qkv
    q_low, k_low, v_low, mixed, lse = attention_forward(lengths, qkv, tables)
    mixed_grad = product(grad_all, w_proj_t).astype(BF16)
    qkv_grad = attention_backward(lengths, q_low, k_low, v_low, mixed_grad, lse, tables)
    head_bias_grad = jnp.sum(qkv_grad, axis=0, dtype=F32)
    attn_line = LineScatter(normed, qkv_grad, grad_all, mixed)
    qkv_grad, mixed, attn_line.other = tie(qkv_grad, mixed, attn_line.other)
    attn_line.finish_pair(normed, qkv_grad, grad_all, mixed)
    far_pack, attn_line.mine = tie(far_pack, attn_line.mine)
    gather = LineGather(far_pack)
    near_full, normed, attn_line.mine = tie(near_full, normed, attn_line.mine)

    def forward(full, low, high):
        w_up, w_down_t = full[:, : high - low], full[:, high - low :]
        act, back = tie(*gelu_pair(product(normed, w_up) + b_up[low:high]))
        return w_up, w_down_t, act, back

    def plus(total, left, right):
        return (total.astype(F32) + times_trans(left, right)).astype(BF16)

    near_up, near_down_t, near_act, back = forward(near_full, edges[0], edges[1])
    near_grad = (product(grad_all, near_down_t) * back.astype(F32)).astype(BF16)
    near_act, near_grad, grad_all = advance([attn_line, gather], near_act, near_grad, grad_all)
    line = LineScatter(normed, near_grad, grad_all, near_act)
    near_act, near_grad, line.other = tie(near_act, near_grad, line.other)
    line.finish_pair(normed, near_grad, grad_all, near_act)
    near_act, line.mine, mixed, qkv_grad = advance(
        [attn_line, gather], near_act, line.mine, mixed, qkv_grad
    )
    branch = times_trans(mixed, w_proj_t).astype(BF16)
    normed_grad = times_trans(qkv_grad, w_qkv).astype(BF16)
    branch, normed_grad, near_act = advance([gather, line], branch, normed_grad, near_act)
    branch = plus(branch, near_act, near_down_t)
    lines = [attn_line, line]
    branch, normed, grad_all, near_grad = advance([gather, attn_line], branch, normed, grad_all, near_grad)
    while not gather.done():
        normed, grad_all = advance([gather], normed, grad_all)
    w_up, w_down_t, act, back = forward(gather.full, edges[1], edges[2])
    up_pre_grad = (product(grad_all, w_down_t) * back.astype(F32)).astype(BF16)
    far_grad = natural_grads(normed, up_pre_grad, grad_all, act)
    far_grad, act, up_pre_grad, near_grad = advance(lines, far_grad, act, up_pre_grad, near_grad)
    far_shard = lax.psum_scatter(far_grad, "dp", scatter_dimension=0, tiled=True)
    branch_low = plus(branch, act, w_down_t)

    output_sum = TensorScatter(branch_low, tok_rows)
    near_grad, branch_low = tie(near_grad, branch_low)
    normed_grad_low = plus(plus(normed_grad, near_grad, near_up), up_pre_grad, w_up)
    (normed_grad_low,) = output_sum.second(normed_grad_low)
    up_bias_grads = [jnp.sum(item, axis=0, dtype=F32) for item in (near_grad, up_pre_grad)]
    grad_sum = TensorScatter(normed_grad_low, tok_rows)
    gain_shift = norm_sums(tensor.astype(jnp.int32)[None], tok_parts, normed_grad_low)
    (gain_shift,) = advance(lines, gain_shift)
    (gain_shift,) = grad_sum.second(gain_shift)
    own = tokens.astype(F32)
    (output_rows,) = output_sum.result()
    output = (own + output_rows + b_out).astype(BF16)
    own_pos = tensor * tok_rows + jnp.arange(tok_rows)
    own_grad = jnp.where((own_pos < slot_len)[:, None], cotangent.astype(F32), 0.0)

    shared = jnp.concatenate([gain_shift.reshape(-1), jnp.sum(own_grad, axis=0)])
    kept = jnp.concatenate([head_bias_grad] + up_bias_grads)
    summed = all_sum(jnp.concatenate([shared, kept]).reshape(-1, LANES), "dp")
    many = shared.shape[0] // LANES
    shared = summed[:many]
    while not all(item.done() for item in lines):
        (shared,) = advance(lines, shared)
    shared = all_sum(shared, "tensor")
    attn_shard = attn_line.total
    mlp_shards = [line.total, far_shard.astype(F32)]
    own_normed_grad, shared = grad_sum.result(shared)
    _, norm_back = jax.vjp(lambda rows: layer_norm(rows, n_gain, n_shift), own)
    input_grad = own_grad + norm_back(own_normed_grad)[0]
    shared = shared.reshape(3, dp_count, shard)
    gain_grad, shift_grad, out_bias = lax.dynamic_index_in_dim(shared, place, 1, keepdims=False)
    kept = summed[many:].reshape(-1)
    head_out = lax.dynamic_index_in_dim(
        kept[: head_bias_grad.shape[0]]
        .reshape(pairs, 3, LANES)
        .transpose(1, 0, 2)
        .reshape(3, heads_here, dp_count, HEAD // dp_count),
        place,
        2,
        keepdims=False,
    )
    up_bias_out = lax.dynamic_index_in_dim(
        kept[head_bias_grad.shape[0] :].reshape(up_bias.shape[0], dp_count, -1), place, 1, keepdims=False
    )

    def part_of(which):
        return jnp.concatenate(
            [attn_shard[:, (3 * p + which) * LANES : (3 * p + which + 1) * LANES] for p in range(pairs)], axis=1
        )

    up_out = jnp.concatenate([item[:, : item.shape[1] // 2] for item in mlp_shards], axis=1)
    down_out = jnp.concatenate([item[:, item.shape[1] // 2 :].T for item in mlp_shards], axis=0)
    return (
        output,
        input_grad,
        gain_grad,
        shift_grad,
        part_of(0),
        part_of(1),
        part_of(2),
        head_out,
        attn_shard[:, in_cols:].T,
        out_bias,
        up_out,
        up_bias_out,
        down_out,
        out_bias,
    )


def solution(mesh):
    rows = P(("dp", "tensor"), None)
    both = P("dp", "tensor")
    turned = P("tensor", "dp")
    heads = P(None, "tensor", "dp")
    vec = P("dp")
    return jax.shard_map(
        on_device,
        mesh=mesh,
        in_specs=(rows, rows, vec, vec, vec, both, both, both, heads, turned, vec, both, turned, turned, vec),
        out_specs=(rows, rows, vec, vec, both, both, both, heads, turned, vec, both, turned, turned, vec),
        check_vma=False,
    )
```

```python
import functools

import jax
import jax.numpy as jnp
from jax import lax
from jax.experimental import pallas as pl
from jax.experimental.pallas import tpu as pltpu
from jax.sharding import PartitionSpec as P

HEAD = 64
ROT = 32
LANES = 128
QBLOCK = 256
MLP_PARTS = (9, 7)

norm_eps = 1e-05
masked_score = -1000000000.0
F32 = jnp.float32
BF16 = jnp.bfloat16


def layer_norm(rows, gain, shift):
    center = rows - jnp.mean(rows, axis=-1, keepdims=True)
    spread = jnp.mean(center * center, axis=-1, keepdims=True)
    return center * lax.rsqrt(spread + norm_eps) * gain + shift


def product(left, right):
    return jnp.dot(left, right, preferred_element_type=F32)


def times_trans(left, right):
    return lax.dot_general(left, right, (((1,), (1,)), ((), ())), preferred_element_type=F32)


def inner_rows(left, right):
    return lax.dot_general(left, right, (((0,), (0,)), ((), ())), preferred_element_type=F32)


def rotary_lanes(count):
    half = ROT // 2
    lane = jnp.arange(LANES) % HEAD
    freq = 1.0 / 10000.0 ** ((lane % half).astype(F32) * (2.0 / ROT))
    angle = jnp.arange(count, dtype=F32)[:, None] * freq[None, :]
    cosine, sine = jnp.cos(angle), jnp.sin(angle)
    keep = jnp.where(lane < ROT, cosine, 1.0)
    from_left = jnp.where((lane >= half) & (lane < ROT), sine, 0.0)
    from_right = jnp.where(lane < half, -sine, 0.0)
    return keep, from_left, from_right


def turn(field, keep, from_left, from_right):
    half = ROT // 2
    left = pltpu.roll(field, half, 1)
    right = pltpu.roll(field, LANES - half, 1)
    return field * keep + left * from_left + right * from_right


def lane_iota(rows):
    return lax.broadcasted_iota(jnp.int32, (rows, LANES), 1)


def attn_fwd_kernel(len_ref, qkv_ref, keep_ref, left_ref, right_ref, q_ref, k_ref, v_ref, mix_ref, lse_ref):
    seq = qkv_ref.shape[0]
    scale = HEAD ** (-0.5)
    slot_len = len_ref[0]
    keep, left, right = keep_ref[...], left_ref[...], right_ref[...]
    q_low = turn(qkv_ref[:, :LANES], keep, left, right).astype(BF16) * jnp.asarray(scale, BF16)
    k_low = turn(qkv_ref[:, LANES : 2 * LANES], keep, left, right).astype(BF16)
    v_low = qkv_ref[:, 2 * LANES :].astype(BF16)
    q_ref[...] = q_low
    k_ref[...] = k_low
    v_ref[...] = v_low
    lane = lane_iota(seq)
    key_row = lax.broadcasted_iota(jnp.int32, (seq, LANES), 0)
    key_bias = jnp.where(key_row < slot_len, 0.0, masked_score).astype(BF16)
    one = jnp.ones((seq, LANES), BF16)
    none = jnp.zeros((seq, LANES), BF16)
    q_heads, k_heads, v_heads = [], [], []
    for head in range(2):
        inside = (lane // HEAD) == head
        flag = lane == (1 - head) * HEAD
        q_heads.append(jnp.where(inside, q_low, jnp.where(flag, one, none)))
        k_heads.append(jnp.where(flag, key_bias, k_low))
        v_heads.append(jnp.where(flag, one, v_low))
    rows = lax.broadcasted_iota(jnp.int32, (QBLOCK, QBLOCK), 0)
    cols = lax.broadcasted_iota(jnp.int32, (QBLOCK, QBLOCK), 1)
    causal = cols <= rows
    lane_q = lane_iota(QBLOCK)
    for block in range(seq // QBLOCK):
        start = block * QBLOCK
        mixed = []
        lses = []
        for head in range(2):
            q_block = q_heads[head][start : start + QBLOCK]
            diag = times_trans(q_block, k_heads[head][start : start + QBLOCK])
            diag = jnp.where(causal, diag, masked_score)
            top = jnp.max(diag, axis=1, keepdims=True)
            if block:
                past = times_trans(q_block, k_heads[head][:start])
                top = jnp.maximum(top, jnp.max(past, axis=1, keepdims=True))
            total = product(jnp.exp(diag - top).astype(BF16), v_heads[head][start : start + QBLOCK])
            if block:
                total += product(jnp.exp(past - top).astype(BF16), v_heads[head][:start])
            flag = (1 - head) * HEAD
            norm = total[:, flag : flag + 1]
            mixed.append(total * (1.0 / norm))
            lses.append(top + jnp.log(norm))
        mix_ref[start : start + QBLOCK, :] = jnp.where(lane_q < HEAD, mixed[0], mixed[1]).astype(BF16)
        lse_ref[start : start + QBLOCK, :] = jnp.where(lane_q < HEAD, lses[0], lses[1])


def attn_bwd_kernel(
    len_ref, q_ref, k_ref, v_ref, grad_ref, lse_ref, keep_ref, left_ref, right_ref, out_ref, dk_ref, dv_ref
):
    seq = q_ref.shape[0]
    scale = HEAD ** (-0.5)
    slot_len = len_ref[0]
    lane = lane_iota(seq)
    key_row = lax.broadcasted_iota(jnp.int32, (seq, LANES), 0)
    key_bias = jnp.where(key_row < slot_len, 0.0, masked_score).astype(BF16)
    none = jnp.zeros((seq, LANES), BF16)
    one = jnp.ones((seq, LANES), BF16)
    k_low = k_ref[...]
    v_low = v_ref[...]
    lane_q = lane_iota(QBLOCK)
    rows = lax.broadcasted_iota(jnp.int32, (QBLOCK, QBLOCK), 0)
    cols = lax.broadcasted_iota(jnp.int32, (QBLOCK, QBLOCK), 1)
    causal = cols <= rows
    k_heads, q_flags, q_clean, g_clean = [], [], [], []
    for head in range(2):
        inside = (lane // HEAD) == head
        flag = lane == (1 - head) * HEAD
        k_heads.append(jnp.where(flag, key_bias, k_low))
        clean = jnp.where(inside, q_ref[...], none)
        q_clean.append(clean)
        q_flags.append(jnp.where(flag, one, clean))
        g_clean.append(jnp.where(inside, grad_ref[...], none))
    blocks = seq // QBLOCK
    for block in range(blocks):
        start = block * QBLOCK
        stop = start + QBLOCK
        parts = []
        for head in range(2):
            lse = lse_ref[start:stop, head * HEAD : head * HEAD + 1]
            q_block = q_clean[head][start:stop]
            g_block = g_clean[head][start:stop]
            spans = [(start, stop)] + ([(0, start)] if block else [])
            kept = []
            row_dot = 0.0
            for low, high in spans:
                logits = times_trans(q_flags[head][start:stop], k_heads[head][low:high])
                if low == start:
                    logits = jnp.where(causal, logits, masked_score)
                probs = jnp.exp(logits - lse)
                prob_grad = times_trans(g_block, v_low[low:high])
                row_dot = row_dot + jnp.sum(probs * prob_grad, axis=1, keepdims=True)
                kept.append((low, high, probs, prob_grad))
            query = 0.0
            for low, high, probs, prob_grad in kept:
                score_grad = (probs * (prob_grad - row_dot)).astype(BF16)
                query = query + product(score_grad, k_low[low:high])
                key_part = inner_rows(score_grad, q_block)
                value_part = inner_rows(probs.astype(BF16), g_block)
                if low == start and head == 0:
                    dk_ref[low:high, :] = key_part
                    dv_ref[low:high, :] = value_part
                else:
                    dk_ref[low:high, :] += key_part
                    dv_ref[low:high, :] += value_part
            parts.append(query)
        query = jnp.where(lane_q < HEAD, parts[0], parts[1]) * scale
        out_ref[start:stop, :LANES] = turn(
            query, keep_ref[start:stop, :], -left_ref[start:stop, :], -right_ref[start:stop, :]
        ).astype(BF16)
    out_ref[:, LANES : 2 * LANES] = turn(
        dk_ref[...], keep_ref[...], -left_ref[...], -right_ref[...]
    ).astype(BF16)
    out_ref[:, 2 * LANES :] = dv_ref[...].astype(BF16)


def attention_forward(lengths, qkv, tables):
    seq, width = qkv.shape
    pairs = width // (3 * LANES)
    wide = pl.BlockSpec((seq, 3 * LANES), lambda p: (0, p))
    col = pl.BlockSpec((seq, LANES), lambda p: (0, p))
    whole = pl.BlockSpec((seq, LANES), lambda p: (0, 0))
    low = jax.ShapeDtypeStruct((seq, pairs * LANES), BF16)
    return pl.pallas_call(
        attn_fwd_kernel,
        grid=(pairs,),
        in_specs=[pl.BlockSpec(memory_space=pltpu.SMEM), wide, whole, whole, whole],
        out_specs=[col] * 5,
        out_shape=[low, low, low, low, jax.ShapeDtypeStruct((seq, pairs * LANES), F32)],
        compiler_params=pltpu.CompilerParams(
            dimension_semantics=("arbitrary",), vmem_limit_bytes=48 * 1024 * 1024
        ),
        cost_estimate=pl.CostEstimate(
            flops=pairs * 12 * seq * seq * LANES, bytes_accessed=pairs * seq * LANES * 24, transcendentals=0
        ),
        name="attn_fwd",
    )(lengths, qkv, *tables)


def attention_backward(lengths, q_low, k_low, v_low, mixed_grad, lse, tables):
    seq = q_low.shape[0]
    pairs = q_low.shape[1] // LANES
    wide = pl.BlockSpec((seq, 3 * LANES), lambda p: (0, p))
    col = pl.BlockSpec((seq, LANES), lambda p: (0, p))
    whole = pl.BlockSpec((seq, LANES), lambda p: (0, 0))
    return pl.pallas_call(
        attn_bwd_kernel,
        grid=(pairs,),
        in_specs=[pl.BlockSpec(memory_space=pltpu.SMEM)] + [col] * 5 + [whole] * 3,
        out_specs=wide,
        out_shape=jax.ShapeDtypeStruct((seq, pairs * 3 * LANES), BF16),
        scratch_shapes=[pltpu.VMEM((seq, LANES), F32), pltpu.VMEM((seq, LANES), F32)],
        compiler_params=pltpu.CompilerParams(
            dimension_semantics=("arbitrary",), vmem_limit_bytes=48 * 1024 * 1024
        ),
        cost_estimate=pl.CostEstimate(
            flops=pairs * 30 * seq * seq * LANES, bytes_accessed=pairs * seq * LANES * 24, transcendentals=0
        ),
        name="attn_bwd",
    )(lengths, q_low, k_low, v_low, mixed_grad, lse, *tables)


def swap_pairs(count, flip):
    return [(i, i ^ flip) for i in range(count)]


def bits_below(count):
    return [1 << b for b in range(count.bit_length() - 1)]


def norm_rows(rows):
    center = rows - jnp.mean(rows, axis=-1, keepdims=True)
    spread = jnp.mean(center * center, axis=-1, keepdims=True)
    return center * lax.rsqrt(spread + norm_eps)


def joined(pieces, low, high):
    return jnp.concatenate([piece[low:high, :].astype(F32) for piece in pieces], axis=1)


def norm_kernel(at_ref, *refs):
    *pieces, gain_ref, shift_ref = refs[:-2]
    out_ref = refs[-1]
    rows = out_ref.shape[0]
    for low in range(0, rows, 32):
        part = norm_rows(joined(pieces, low, low + 32))
        out_ref[low : low + 32, :] = (part * gain_ref[...] + shift_ref[...]).astype(BF16)


def mask_kernel(at_ref, len_ref, *refs):
    pieces = refs[:-2]
    out_ref = refs[-1]
    rows, width = out_ref.shape
    pos = at_ref[0] * rows + lax.broadcasted_iota(jnp.int32, (rows, width), 0)
    whole = jnp.concatenate([piece[...] for piece in pieces], axis=1)
    out_ref[...] = jnp.where(pos < len_ref[0], whole, jnp.zeros_like(whole))


def place_rows(kernel, name, seq_rows, pieces, extra, scalars, buffer):
    tok_rows = pieces[0].shape[0]
    width = sum(piece.shape[1] for piece in pieces)
    count = len(scalars)
    whole = lambda item: pl.BlockSpec(item.shape, lambda i, *s: (0, 0))
    last = [] if buffer is None else [buffer]
    operands = list(pieces) + list(extra) + (last or [extra[0] if extra else pieces[0]])
    specs = [whole(item) for item in list(pieces) + list(extra)] + [pl.BlockSpec(memory_space=pl.ANY)]
    return pl.pallas_call(
        kernel,
        grid_spec=pltpu.PrefetchScalarGridSpec(
            num_scalar_prefetch=count,
            grid=(1,),
            in_specs=specs,
            out_specs=pl.BlockSpec((tok_rows, width), lambda i, at, *s: (at[0], 0)),
        ),
        out_shape=jax.ShapeDtypeStruct((seq_rows, width), BF16),
        input_output_aliases={count + len(operands) - 1: 0} if last else {},
        name=name,
    )(*scalars, *operands)


def sums_kernel(counts, at_ref, *refs):
    parts, (grad_ref, out_ref, gain_acc, shift_acc) = list(refs[:-4]), refs[-4:]
    rows = parts[0].shape[0]
    gain_acc[...] = jnp.zeros_like(gain_acc)
    shift_acc[...] = jnp.zeros_like(shift_acc)
    step = gain_acc.shape[0]
    for flip, count in enumerate(counts):
        pieces = [parts.pop(0) for _ in range(count)]
        base = pl.multiple_of((at_ref[0] ^ flip) * rows, rows)
        for low in range(0, rows, step):
            grad = grad_ref[pl.ds(base + low, step), :].astype(F32)
            gain_acc[...] += grad * norm_rows(joined(pieces, low, low + step))
            shift_acc[...] += grad
    out_ref[0:1, :] = jnp.sum(gain_acc[...], axis=0, keepdims=True)
    out_ref[1:2, :] = jnp.sum(shift_acc[...], axis=0, keepdims=True)


def norm_sums(tensor, parts, grad):
    width = grad.shape[1]
    pieces = [piece for part in parts for piece in part]
    vmem = pl.BlockSpec(memory_space=pltpu.VMEM)
    return pl.pallas_call(
        functools.partial(sums_kernel, [len(part) for part in parts]),
        in_specs=[pl.BlockSpec(memory_space=pltpu.SMEM)] + [vmem] * (len(pieces) + 1),
        out_specs=vmem,
        out_shape=jax.ShapeDtypeStruct((2, width), F32),
        scratch_shapes=[pltpu.VMEM((32, width), F32), pltpu.VMEM((32, width), F32)],
        compiler_params=pltpu.CompilerParams(vmem_limit_bytes=32 * 1024 * 1024),
        cost_estimate=pl.CostEstimate(flops=16 * grad.size, bytes_accessed=4 * grad.size, transcendentals=0),
        name="norm_sums",
    )(tensor, *pieces, grad)


def weight_kernel(at_ref, left_a, right_a, left_b, right_b, out_ref):
    width = right_a.shape[1]
    out_ref[:, :width] = inner_rows(left_a[...], right_a[...]).astype(BF16)
    out_ref[:, width:] = inner_rows(left_b[...], right_b[...]).astype(BF16)


def weight_grads(left_a, right_a, left_b, right_b, first, stride, blocks, rows):
    seq = left_a.shape[0]
    width = right_a.shape[1] + right_b.shape[1]
    block = pl.BlockSpec((seq, rows), lambda i, at: (0, stride * i + at[0]))
    whole = lambda item: pl.BlockSpec(item.shape, lambda i, at: (0, 0))
    return pl.pallas_call(
        weight_kernel,
        grid_spec=pltpu.PrefetchScalarGridSpec(
            num_scalar_prefetch=1,
            grid=(blocks,),
            in_specs=[block, whole(right_a), block, whole(right_b)],
            out_specs=pl.BlockSpec((rows, width), lambda i, at: (i, 0)),
        ),
        out_shape=jax.ShapeDtypeStruct((blocks * rows, width), BF16),
        compiler_params=pltpu.CompilerParams(vmem_limit_bytes=32 * 1024 * 1024),
        cost_estimate=pl.CostEstimate(
            flops=2 * seq * blocks * rows * width,
            bytes_accessed=2 * seq * (width + 2 * blocks * rows) + 2 * blocks * rows * width,
            transcendentals=0,
        ),
        name="weight_grads",
    )(first, left_a, right_a, left_b, right_b)


def tie(*values):
    return lax.optimization_barrier(values)


class LineScatter:
    def __init__(self, left_a, right_a, left_b, right_b):
        self.size = lax.axis_size("dp")
        self.stations = self.size // 2
        me = lax.axis_index("dp")
        self.core, self.place = me % 2, me // 2
        self.rows = left_a.shape[1] // self.size
        self.other = weight_grads(
            left_a, right_a, left_b, right_b, (1 - self.core)[None], 2, self.stations, self.rows
        )
        self.step = 0

    def finish_pair(self, left_a, right_a, left_b, right_b):
        self.mine = weight_grads(
            left_a, right_a, left_b, right_b, self.core[None], 2, self.stations, self.rows
        )
        self.held = (lax.ppermute(self.other, "dp", swap_pairs(self.size, 1)),)

    def at(self, target):
        target = jnp.clip(target, 0, self.stations - 1)
        pick = lambda item: lax.dynamic_slice_in_dim(item, target * self.rows, self.rows, 0).astype(F32)
        return pick(self.mine) + pick(self.got)

    def next_sends(self):
        if self.step == 0:
            (self.got,) = self.held
            self.held = (None, None)
        self.step += 1
        if self.step >= self.stations:
            up, down = self.held
            self.total = self.at(self.place) + up.astype(F32) + down.astype(F32)
            return ()
        up, down = self.held if len(self.held) == 2 else self.held * 2
        above = self.place + self.stations - self.step
        below = self.place - self.stations + self.step
        add = lambda sent, item: (sent if item is None else sent + item.astype(F32)).astype(BF16)
        if 2 * self.step < self.stations - 1:
            near = 2 * self.place < self.stations
            sent = self.at(jnp.where(near, above, below))
            return (add(sent, up),)
        return add(self.at(above), up), add(self.at(below), down)

    def send(self, sends):
        to_up = [(2 * z + c, 2 * z + 2 + c) for z in range(self.step) for c in range(2)]
        to_down = [(self.size - 1 - a, self.size - 1 - b) for a, b in to_up]
        if len(sends) == 1:
            self.held = (lax.ppermute(sends[0], "dp", to_up + to_down),)
        else:
            self.held = tuple(lax.ppermute(item, "dp", way) for item, way in zip(sends, (to_up, to_down)))

    def done(self):
        return self.step >= self.stations


def weave_kernel(at_ref, mine_ref, got_ref, out_ref):
    same = pl.program_id(0) % 2 == at_ref[1]

    @pl.when(same)
    def _():
        out_ref[...] = mine_ref[...]

    @pl.when(jnp.logical_not(same))
    def _():
        out_ref[...] = got_ref[...]


class LineGather:
    def __init__(self, pack):
        self.size = lax.axis_size("dp")
        self.stations = self.size // 2
        me = lax.axis_index("dp")
        self.core, self.place = me % 2, me // 2
        self.pack = pack
        self.step = 1
        self.came = []
        self.send((pack, pack))

    def send(self, sends):
        if self.step == self.stations:
            self.held = (lax.ppermute(sends[0], "dp", swap_pairs(self.size, 1)),)
            return
        to_up = [(2 * z + c, 2 * z + 2 + c) for z in range(self.step - 1, self.stations - 1) for c in range(2)]
        to_down = [(self.size - 1 - a, self.size - 1 - b) for a, b in to_up]
        if len(sends) == 1:
            self.held = (lax.ppermute(sends[0], "dp", to_up + to_down),)
        else:
            self.held = tuple(lax.ppermute(item, "dp", way) for item, way in zip(sends, (to_up, to_down)))

    def next_sends(self):
        self.step += 1
        if self.step == self.stations + 1:
            self.full = self.weave(self.stack, self.held[0])
            return ()
        up, down = self.held if len(self.held) == 2 else self.held * 2
        self.came.append((up, down))
        if self.step == self.stations:
            parts = [self.pack]
            for far in range(1, self.stations):
                ahead = self.place + far < self.stations
                parts.append(jnp.where(ahead, self.came[far - 1][1], self.came[self.stations - far - 1][0]))
            self.stack = jnp.concatenate(parts)
            return (self.stack,)
        if 2 * self.step > self.stations + 1:
            return (jnp.where(2 * self.place >= self.stations, up, down),)
        return up, down

    def weave(self, mine, got):
        rows, width = self.pack.shape
        stations = self.stations
        half = pl.BlockSpec((rows, width), lambda i, at: ((i // 2 + stations - at[0]) % stations, 0))
        return pl.pallas_call(
            weave_kernel,
            grid_spec=pltpu.PrefetchScalarGridSpec(
                num_scalar_prefetch=1,
                grid=(self.size,),
                in_specs=[half, half],
                out_specs=pl.BlockSpec((rows, width), lambda i, at: (i, 0)),
            ),
            out_shape=jax.ShapeDtypeStruct((self.size * rows, width), BF16),
            cost_estimate=pl.CostEstimate(
                flops=0, bytes_accessed=6 * self.size * rows * width, transcendentals=0
            ),
            name="weave",
        )(jnp.stack([self.place, self.core]).astype(jnp.int32), mine, got)

    def done(self):
        return self.step > self.stations


def advance(lines, *values):
    lines = [line for line in lines if not line.done()]
    flat = tie(*[item for line in lines for item in line.held], *values)
    for line in lines:
        line.held, flat = flat[: len(line.held)], flat[len(line.held) :]
    sends = [line.next_sends() for line in lines]
    flat = tie(*[item for sent in sends for item in sent], *flat)
    for line, sent in zip(lines, sends):
        if sent:
            line.send(flat[: len(sent)])
            flat = flat[len(sent) :]
    return flat


def natural_grads(left_a, right_a, left_b, right_b):
    size = lax.axis_size("dp")
    zero = jnp.zeros((1,), jnp.int32)
    return weight_grads(left_a, right_a, left_b, right_b, zero, 1, size, left_a.shape[1] // size)


class TensorScatter:
    def __init__(self, partial, tok_rows):
        self.count = lax.axis_size("tensor")
        tensor = lax.axis_index("tensor")
        half = partial.shape[1] // 2

        def block(flip, side):
            start = ((tensor ^ flip) * tok_rows, side * half)
            return lax.dynamic_slice(partial, start, (tok_rows, half))

        self.block, self.tok_rows = block, tok_rows
        self.rest = []
        if self.count > 4:
            self.rest = [
                lax.ppermute(block(flip, side), "tensor", swap_pairs(self.count, flip))
                for side in (0, 1)
                for flip in range(1, self.count)
            ]
            return
        self.first = []
        for side, flip in ((0, 1), (1, 2)):
            sent = jnp.concatenate([block(flip, side), block(3, side)])
            self.first.append(lax.ppermute(sent, "tensor", swap_pairs(self.count, flip)))

    def second(self, *values):
        if self.count > 4:
            return values
        self.total = []
        flat = tie(*self.first, *values)
        self.first, values = flat[:2], flat[2:]
        for side, flip in ((0, 1), (1, 2)):
            got = self.first[side].astype(F32)
            far = (self.block(3 - flip, side).astype(F32) + got[self.tok_rows :]).astype(BF16)
            near = self.block(0, side).astype(F32) + got[: self.tok_rows]
            self.total.append((near, lax.ppermute(far, "tensor", swap_pairs(self.count, 3 - flip))))
        return values

    def result(self, *values):
        if self.count > 4:
            flat = tie(*self.rest, *values)
            many = self.count - 1
            total = [
                sum((item.astype(F32) for item in flat[side * many : (side + 1) * many]), self.block(0, side).astype(F32))
                for side in (0, 1)
            ]
            return (jnp.concatenate(total, axis=1),) + flat[2 * many :]
        flat = tie(*[item for _, item in self.total], *values)
        total = [near + item.astype(F32) for (near, _), item in zip(self.total, flat)]
        return (jnp.concatenate(total, axis=1),) + flat[2:]


def all_sum(value, axis):
    count = lax.axis_size(axis)
    for bit in bits_below(count):
        value = value + lax.ppermute(value, axis, swap_pairs(count, bit))
    return value


def gelu_pair(value):
    slope = (2.0 / jnp.pi) ** 0.5
    square = value * value
    flat = jnp.tanh(slope * value * (1.0 + 0.044715 * square))
    act = 0.5 * value * (1.0 + flat)
    back = 0.5 * (1.0 + flat) + 0.5 * value * (1.0 - flat * flat) * slope * (1.0 + 3 * 0.044715 * square)
    return act.astype(BF16), back.astype(BF16)


def on_device(
    tokens,
    cotangent,
    lengths,
    norm_gain,
    norm_bias,
    query_weight,
    key_weight,
    value_weight,
    qkv_bias,
    proj_weight,
    proj_bias,
    up_weight,
    up_bias,
    down_weight,
    down_bias,
):
    tensor_count = lax.axis_size("tensor")
    dp_count = lax.axis_size("dp")
    tensor = lax.axis_index("tensor")
    place = lax.axis_index("dp")
    tok_rows, width = tokens.shape
    seq_rows = tok_rows * tensor_count
    heads_width = query_weight.shape[1]
    ff = up_weight.shape[1]
    pairs = heads_width // LANES
    slot_len = lengths[0]

    small = jnp.concatenate(
        [norm_gain, norm_bias, proj_bias, down_bias, qkv_bias.reshape(-1), up_bias.reshape(-1)]
    )
    mine_row = (jnp.arange(dp_count) == place)[:, None]
    small_all = all_sum(jnp.where(mine_row, small[None, :], jnp.zeros((), BF16)), "dp")
    shard = norm_gain.shape[0]
    b_out = (
        small_all[:, 2 * shard : 3 * shard].astype(F32) + small_all[:, 3 * shard : 4 * shard].astype(F32)
    ).reshape(-1)
    heads_here = qkv_bias.shape[1]
    head_size = qkv_bias.size
    b_heads = (
        small_all[:, 4 * shard : 4 * shard + head_size]
        .reshape((dp_count,) + qkv_bias.shape)
        .transpose(1, 2, 0, 3)
        .reshape(3, pairs, LANES)
    )
    b_qkv = b_heads.transpose(1, 0, 2).reshape(-1).astype(F32)
    b_up = (
        small_all[:, 4 * shard + head_size :]
        .reshape((dp_count,) + up_bias.shape)
        .transpose(1, 0, 2)
        .reshape(-1)
        .astype(F32)
    )

    down_t = down_weight.T
    weight_sum = sum(MLP_PARTS)
    edges = [0]
    for part in MLP_PARTS:
        edges.append(edges[-1] + ff * part // weight_sum)

    def mlp_pack(index):
        low, high = edges[index], edges[index + 1]
        return jnp.concatenate([up_weight[:, low:high], down_t[:, low:high]], axis=1)

    attn_in = [
        item[:, p * LANES : (p + 1) * LANES]
        for p in range(pairs)
        for item in (query_weight, key_weight, value_weight)
    ]
    attn_pack = jnp.concatenate(attn_in + [proj_weight.T], axis=1)
    attn_full = lax.all_gather(attn_pack, "dp", axis=0, tiled=True)
    near_pack, far_pack = mlp_pack(0), mlp_pack(1)

    half = width // 2

    def direct(rows, flip):
        return lax.ppermute(rows, "tensor", swap_pairs(tensor_count, flip))

    def third(first, second):
        return [direct(first[:, :half], 2), direct(second[:, half:], 1)]

    tok_one, tok_two, small_all = tie(direct(tokens, 1), direct(tokens, 2), small_all)
    tok_one, near_pack = tie(tok_one, near_pack)
    near_full = lax.all_gather(near_pack, "dp", axis=0, tiled=True)
    tok_three = third(tok_one, tok_two)
    cot_held, tok_one, tok_two = tie(cotangent, tok_one, tok_two)
    cot_one, cot_two = direct(cot_held, 1), direct(cot_held, 2)
    more = range(4, tensor_count)
    tok_more = [[direct(tokens, flip)] for flip in more]

    n_gain = small_all[:, :shard].reshape(-1).astype(F32)
    n_shift = small_all[:, shard : 2 * shard].reshape(-1).astype(F32)

    def where_of(flip):
        return (tensor ^ flip).astype(jnp.int32)[None]

    gain_row, shift_row = n_gain[None, :], n_shift[None, :]
    tok_parts = [[tokens], [tok_one], [tok_two], tok_three] + tok_more
    normed = None
    for flip in range(tensor_count):
        if flip == 3:
            normed, cot_one, cot_two = tie(normed, cot_one, cot_two)
            cot_three = third(cot_one, cot_two)
        normed = place_rows(
            norm_kernel, "norm_rows", seq_rows, tok_parts[flip], [gain_row, shift_row], [where_of(flip)], normed
        )
    cot_parts = [[cotangent], [cot_one], [cot_two], cot_three] + [[direct(cot_held, flip)] for flip in more]
    grad_all = None
    for flip in range(tensor_count):
        grad_all = place_rows(
            mask_kernel, "mask_rows", seq_rows, cot_parts[flip], [], [where_of(flip), lengths], grad_all
        )
    normed, grad_all, far_pack = tie(normed, grad_all, far_pack)

    tables = rotary_lanes(seq_rows)
    in_cols = 3 * heads_width
    w_qkv = attn_full[:, :in_cols]
    w_proj_t = attn_full[:, in_cols:]
    qkv = product(normed, w_qkv) + b_qkv
    q_low, k_low, v_low, mixed, lse = attention_forward(lengths, qkv, tables)
    mixed_grad = product(grad_all, w_proj_t).astype(BF16)
    qkv_grad = attention_backward(lengths, q_low, k_low, v_low, mixed_grad, lse, tables)
    head_bias_grad = jnp.sum(qkv_grad, axis=0, dtype=F32)
    attn_line = LineScatter(normed, qkv_grad, grad_all, mixed)
    qkv_grad, mixed, attn_line.other = tie(qkv_grad, mixed, attn_line.other)
    attn_line.finish_pair(normed, qkv_grad, grad_all, mixed)
    far_pack, attn_line.mine = tie(far_pack, attn_line.mine)
    gather = LineGather(far_pack)
    near_full, normed, attn_line.mine = tie(near_full, normed, attn_line.mine)

    def forward(full, low, high):
        w_up, w_down_t = full[:, : high - low], full[:, high - low :]
        act, back = tie(*gelu_pair(product(normed, w_up) + b_up[low:high]))
        return w_up, w_down_t, act, back

    def plus(total, left, right):
        return (total.astype(F32) + times_trans(left, right)).astype(BF16)

    near_up, near_down_t, near_act, back = forward(near_full, edges[0], edges[1])
    near_grad = (product(grad_all, near_down_t) * back.astype(F32)).astype(BF16)
    near_act, near_grad, grad_all = advance([attn_line, gather], near_act, near_grad, grad_all)
    line = LineScatter(normed, near_grad, grad_all, near_act)
    near_act, near_grad, line.other = tie(near_act, near_grad, line.other)
    line.finish_pair(normed, near_grad, grad_all, near_act)
    near_act, line.mine, mixed, qkv_grad = advance(
        [attn_line, gather], near_act, line.mine, mixed, qkv_grad
    )
    branch = times_trans(mixed, w_proj_t).astype(BF16)
    normed_grad = times_trans(qkv_grad, w_qkv).astype(BF16)
    branch, normed_grad, near_act = advance([gather, line], branch, normed_grad, near_act)
    branch = plus(branch, near_act, near_down_t)
    lines = [attn_line, line]
    branch, normed, grad_all, near_grad = advance([gather, attn_line], branch, normed, grad_all, near_grad)
    while not gather.done():
        normed, grad_all = advance([gather], normed, grad_all)
    w_up, w_down_t, act, back = forward(gather.full, edges[1], edges[2])
    up_pre_grad = (product(grad_all, w_down_t) * back.astype(F32)).astype(BF16)
    far_grad = natural_grads(normed, up_pre_grad, grad_all, act)
    far_grad, act, up_pre_grad, near_grad = advance(lines, far_grad, act, up_pre_grad, near_grad)
    far_shard = lax.psum_scatter(far_grad, "dp", scatter_dimension=0, tiled=True)
    branch_low = plus(branch, act, w_down_t)

    output_sum = TensorScatter(branch_low, tok_rows)
    near_grad, branch_low = tie(near_grad, branch_low)
    normed_grad_low = plus(plus(normed_grad, near_grad, near_up), up_pre_grad, w_up)
    (normed_grad_low,) = output_sum.second(normed_grad_low)
    up_bias_grads = [jnp.sum(item, axis=0, dtype=F32) for item in (near_grad, up_pre_grad)]
    grad_sum = TensorScatter(normed_grad_low, tok_rows)
    (normed_grad_low,) = advance(lines, normed_grad_low)
    gain_shift = norm_sums(tensor.astype(jnp.int32)[None], tok_parts, normed_grad_low)
    (gain_shift,) = grad_sum.second(gain_shift)
    own = tokens.astype(F32)
    (output_rows,) = output_sum.result()
    output = (own + output_rows + b_out).astype(BF16)
    own_pos = tensor * tok_rows + jnp.arange(tok_rows)
    own_grad = jnp.where((own_pos < slot_len)[:, None], cotangent.astype(F32), 0.0)

    shared = jnp.concatenate([gain_shift.reshape(-1), jnp.sum(own_grad, axis=0)])
    kept = jnp.concatenate([head_bias_grad] + up_bias_grads)
    shared = all_sum(shared.reshape(-1, LANES), "tensor")
    while not all(item.done() for item in lines):
        (shared,) = advance(lines, shared)
    many = shared.shape[0]
    summed = jnp.concatenate([shared, kept.reshape(-1, LANES)])
    attn_shard = attn_line.total
    mlp_shards = [line.total, far_shard.astype(F32)]
    up_out = jnp.concatenate([item[:, : item.shape[1] // 2] for item in mlp_shards], axis=1)
    down_out = jnp.concatenate([item[:, item.shape[1] // 2 :].T for item in mlp_shards], axis=0)
    (own_normed_grad,) = grad_sum.result()
    _, norm_back = jax.vjp(lambda rows: layer_norm(rows, n_gain, n_shift), own)
    input_grad = own_grad + norm_back(own_normed_grad)[0]
    summed, input_grad, up_out, down_out = tie(summed, input_grad, up_out, down_out)
    summed = all_sum(summed, "dp")
    shared = summed[:many].reshape(3, dp_count, shard)
    gain_grad, shift_grad, out_bias = lax.dynamic_index_in_dim(shared, place, 1, keepdims=False)
    kept = summed[many:].reshape(-1)
    head_out = lax.dynamic_index_in_dim(
        kept[: head_bias_grad.shape[0]]
        .reshape(pairs, 3, LANES)
        .transpose(1, 0, 2)
        .reshape(3, heads_here, dp_count, HEAD // dp_count),
        place,
        2,
        keepdims=False,
    )
    up_bias_out = lax.dynamic_index_in_dim(
        kept[head_bias_grad.shape[0] :].reshape(up_bias.shape[0], dp_count, -1), place, 1, keepdims=False
    )

    def part_of(which):
        return jnp.concatenate(
            [attn_shard[:, (3 * p + which) * LANES : (3 * p + which + 1) * LANES] for p in range(pairs)], axis=1
        )

    return (
        output,
        input_grad,
        gain_grad,
        shift_grad,
        part_of(0),
        part_of(1),
        part_of(2),
        head_out,
        attn_shard[:, in_cols:].T,
        out_bias,
        up_out,
        up_bias_out,
        down_out,
        out_bias,
    )


def solution(mesh):
    rows = P(("dp", "tensor"), None)
    both = P("dp", "tensor")
    turned = P("tensor", "dp")
    heads = P(None, "tensor", "dp")
    vec = P("dp")
    return jax.shard_map(
        on_device,
        mesh=mesh,
        in_specs=(rows, rows, vec, vec, vec, both, both, both, heads, turned, vec, both, turned, turned, vec),
        out_specs=(rows, rows, vec, vec, both, both, both, heads, turned, vec, both, turned, turned, vec),
        check_vma=False,
    )
```

```python
import functools

import jax
import jax.numpy as jnp
from jax import lax
from jax.experimental import pallas as pl
from jax.experimental.pallas import tpu as pltpu
from jax.sharding import PartitionSpec as P

HEAD = 64
ROT = 32
LANES = 128
QBLOCK = 256
MLP_PARTS = (9, 7)

norm_eps = 1e-05
masked_score = -1000000000.0
F32 = jnp.float32
BF16 = jnp.bfloat16


def layer_norm(rows, gain, shift):
    center = rows - jnp.mean(rows, axis=-1, keepdims=True)
    spread = jnp.mean(center * center, axis=-1, keepdims=True)
    return center * lax.rsqrt(spread + norm_eps) * gain + shift


def product(left, right):
    return jnp.dot(left, right, preferred_element_type=F32)


def times_trans(left, right):
    return lax.dot_general(left, right, (((1,), (1,)), ((), ())), preferred_element_type=F32)


def inner_rows(left, right):
    return lax.dot_general(left, right, (((0,), (0,)), ((), ())), preferred_element_type=F32)


def rotary_lanes(count):
    half = ROT // 2
    lane = jnp.arange(LANES) % HEAD
    freq = 1.0 / 10000.0 ** ((lane % half).astype(F32) * (2.0 / ROT))
    angle = jnp.arange(count, dtype=F32)[:, None] * freq[None, :]
    cosine, sine = jnp.cos(angle), jnp.sin(angle)
    keep = jnp.where(lane < ROT, cosine, 1.0)
    from_left = jnp.where((lane >= half) & (lane < ROT), sine, 0.0)
    from_right = jnp.where(lane < half, -sine, 0.0)
    return keep, from_left, from_right


def turn(field, keep, from_left, from_right):
    half = ROT // 2
    left = pltpu.roll(field, half, 1)
    right = pltpu.roll(field, LANES - half, 1)
    return field * keep + left * from_left + right * from_right


def lane_iota(rows):
    return lax.broadcasted_iota(jnp.int32, (rows, LANES), 1)


def attn_fwd_kernel(len_ref, qkv_ref, keep_ref, left_ref, right_ref, q_ref, k_ref, v_ref, mix_ref, lse_ref):
    seq = qkv_ref.shape[0]
    scale = HEAD ** (-0.5)
    slot_len = len_ref[0]
    keep, left, right = keep_ref[...], left_ref[...], right_ref[...]
    q_low = turn(qkv_ref[:, :LANES], keep, left, right).astype(BF16) * jnp.asarray(scale, BF16)
    k_low = turn(qkv_ref[:, LANES : 2 * LANES], keep, left, right).astype(BF16)
    v_low = qkv_ref[:, 2 * LANES :].astype(BF16)
    q_ref[...] = q_low
    k_ref[...] = k_low
    v_ref[...] = v_low
    lane = lane_iota(seq)
    key_row = lax.broadcasted_iota(jnp.int32, (seq, LANES), 0)
    key_bias = jnp.where(key_row < slot_len, 0.0, masked_score).astype(BF16)
    one = jnp.ones((seq, LANES), BF16)
    none = jnp.zeros((seq, LANES), BF16)
    q_heads, k_heads, v_heads = [], [], []
    for head in range(2):
        inside = (lane // HEAD) == head
        flag = lane == (1 - head) * HEAD
        q_heads.append(jnp.where(inside, q_low, jnp.where(flag, one, none)))
        k_heads.append(jnp.where(flag, key_bias, k_low))
        v_heads.append(jnp.where(flag, one, v_low))
    rows = lax.broadcasted_iota(jnp.int32, (QBLOCK, QBLOCK), 0)
    cols = lax.broadcasted_iota(jnp.int32, (QBLOCK, QBLOCK), 1)
    causal = cols <= rows
    lane_q = lane_iota(QBLOCK)
    for block in range(seq // QBLOCK):
        start = block * QBLOCK
        mixed = []
        lses = []
        for head in range(2):
            q_block = q_heads[head][start : start + QBLOCK]
            diag = times_trans(q_block, k_heads[head][start : start + QBLOCK])
            diag = jnp.where(causal, diag, masked_score)
            top = jnp.max(diag, axis=1, keepdims=True)
            if block:
                past = times_trans(q_block, k_heads[head][:start])
                top = jnp.maximum(top, jnp.max(past, axis=1, keepdims=True))
            total = product(jnp.exp(diag - top).astype(BF16), v_heads[head][start : start + QBLOCK])
            if block:
                total += product(jnp.exp(past - top).astype(BF16), v_heads[head][:start])
            flag = (1 - head) * HEAD
            norm = total[:, flag : flag + 1]
            mixed.append(total * (1.0 / norm))
            lses.append(top + jnp.log(norm))
        mix_ref[start : start + QBLOCK, :] = jnp.where(lane_q < HEAD, mixed[0], mixed[1]).astype(BF16)
        lse_ref[start : start + QBLOCK, :] = jnp.where(lane_q < HEAD, lses[0], lses[1])


def attn_bwd_kernel(
    len_ref, q_ref, k_ref, v_ref, grad_ref, lse_ref, keep_ref, left_ref, right_ref, out_ref, dk_ref, dv_ref
):
    seq = q_ref.shape[0]
    scale = HEAD ** (-0.5)
    slot_len = len_ref[0]
    lane = lane_iota(seq)
    key_row = lax.broadcasted_iota(jnp.int32, (seq, LANES), 0)
    key_bias = jnp.where(key_row < slot_len, 0.0, masked_score).astype(BF16)
    none = jnp.zeros((seq, LANES), BF16)
    one = jnp.ones((seq, LANES), BF16)
    k_low = k_ref[...]
    v_low = v_ref[...]
    lane_q = lane_iota(QBLOCK)
    rows = lax.broadcasted_iota(jnp.int32, (QBLOCK, QBLOCK), 0)
    cols = lax.broadcasted_iota(jnp.int32, (QBLOCK, QBLOCK), 1)
    causal = cols <= rows
    k_heads, q_flags, q_clean, g_clean = [], [], [], []
    for head in range(2):
        inside = (lane // HEAD) == head
        flag = lane == (1 - head) * HEAD
        k_heads.append(jnp.where(flag, key_bias, k_low))
        clean = jnp.where(inside, q_ref[...], none)
        q_clean.append(clean)
        q_flags.append(jnp.where(flag, one, clean))
        g_clean.append(jnp.where(inside, grad_ref[...], none))
    blocks = seq // QBLOCK
    for block in range(blocks):
        start = block * QBLOCK
        stop = start + QBLOCK
        parts = []
        for head in range(2):
            lse = lse_ref[start:stop, head * HEAD : head * HEAD + 1]
            q_block = q_clean[head][start:stop]
            g_block = g_clean[head][start:stop]
            spans = [(start, stop)] + ([(0, start)] if block else [])
            kept = []
            row_dot = 0.0
            for low, high in spans:
                logits = times_trans(q_flags[head][start:stop], k_heads[head][low:high])
                if low == start:
                    logits = jnp.where(causal, logits, masked_score)
                probs = jnp.exp(logits - lse)
                prob_grad = times_trans(g_block, v_low[low:high])
                row_dot = row_dot + jnp.sum(probs * prob_grad, axis=1, keepdims=True)
                kept.append((low, high, probs, prob_grad))
            query = 0.0
            for low, high, probs, prob_grad in kept:
                score_grad = (probs * (prob_grad - row_dot)).astype(BF16)
                query = query + product(score_grad, k_low[low:high])
                key_part = inner_rows(score_grad, q_block)
                value_part = inner_rows(probs.astype(BF16), g_block)
                if low == start and head == 0:
                    dk_ref[low:high, :] = key_part
                    dv_ref[low:high, :] = value_part
                else:
                    dk_ref[low:high, :] += key_part
                    dv_ref[low:high, :] += value_part
            parts.append(query)
        query = jnp.where(lane_q < HEAD, parts[0], parts[1]) * scale
        out_ref[start:stop, :LANES] = turn(
            query, keep_ref[start:stop, :], -left_ref[start:stop, :], -right_ref[start:stop, :]
        ).astype(BF16)
    out_ref[:, LANES : 2 * LANES] = turn(
        dk_ref[...], keep_ref[...], -left_ref[...], -right_ref[...]
    ).astype(BF16)
    out_ref[:, 2 * LANES :] = dv_ref[...].astype(BF16)


def attention_forward(lengths, qkv, tables):
    seq, width = qkv.shape
    pairs = width // (3 * LANES)
    wide = pl.BlockSpec((seq, 3 * LANES), lambda p: (0, p))
    col = pl.BlockSpec((seq, LANES), lambda p: (0, p))
    whole = pl.BlockSpec((seq, LANES), lambda p: (0, 0))
    low = jax.ShapeDtypeStruct((seq, pairs * LANES), BF16)
    return pl.pallas_call(
        attn_fwd_kernel,
        grid=(pairs,),
        in_specs=[pl.BlockSpec(memory_space=pltpu.SMEM), wide, whole, whole, whole],
        out_specs=[col] * 5,
        out_shape=[low, low, low, low, jax.ShapeDtypeStruct((seq, pairs * LANES), F32)],
        compiler_params=pltpu.CompilerParams(
            dimension_semantics=("arbitrary",), vmem_limit_bytes=48 * 1024 * 1024
        ),
        cost_estimate=pl.CostEstimate(
            flops=pairs * 12 * seq * seq * LANES, bytes_accessed=pairs * seq * LANES * 24, transcendentals=0
        ),
        name="attn_fwd",
    )(lengths, qkv, *tables)


def attention_backward(lengths, q_low, k_low, v_low, mixed_grad, lse, tables):
    seq = q_low.shape[0]
    pairs = q_low.shape[1] // LANES
    wide = pl.BlockSpec((seq, 3 * LANES), lambda p: (0, p))
    col = pl.BlockSpec((seq, LANES), lambda p: (0, p))
    whole = pl.BlockSpec((seq, LANES), lambda p: (0, 0))
    return pl.pallas_call(
        attn_bwd_kernel,
        grid=(pairs,),
        in_specs=[pl.BlockSpec(memory_space=pltpu.SMEM)] + [col] * 5 + [whole] * 3,
        out_specs=wide,
        out_shape=jax.ShapeDtypeStruct((seq, pairs * 3 * LANES), BF16),
        scratch_shapes=[pltpu.VMEM((seq, LANES), F32), pltpu.VMEM((seq, LANES), F32)],
        compiler_params=pltpu.CompilerParams(
            dimension_semantics=("arbitrary",), vmem_limit_bytes=48 * 1024 * 1024
        ),
        cost_estimate=pl.CostEstimate(
            flops=pairs * 30 * seq * seq * LANES, bytes_accessed=pairs * seq * LANES * 24, transcendentals=0
        ),
        name="attn_bwd",
    )(lengths, q_low, k_low, v_low, mixed_grad, lse, *tables)


def swap_pairs(count, flip):
    return [(i, i ^ flip) for i in range(count)]


def bits_below(count):
    return [1 << b for b in range(count.bit_length() - 1)]


def norm_rows(rows):
    center = rows - jnp.mean(rows, axis=-1, keepdims=True)
    spread = jnp.mean(center * center, axis=-1, keepdims=True)
    return center * lax.rsqrt(spread + norm_eps)


def joined(pieces, low, high):
    return jnp.concatenate([piece[low:high, :].astype(F32) for piece in pieces], axis=1)


def norm_kernel(at_ref, *refs):
    *pieces, gain_ref, shift_ref = refs[:-2]
    out_ref = refs[-1]
    rows = out_ref.shape[0]
    for low in range(0, rows, 32):
        part = norm_rows(joined(pieces, low, low + 32))
        out_ref[low : low + 32, :] = (part * gain_ref[...] + shift_ref[...]).astype(BF16)


def mask_kernel(at_ref, len_ref, *refs):
    pieces = refs[:-2]
    out_ref = refs[-1]
    rows, width = out_ref.shape
    pos = at_ref[0] * rows + lax.broadcasted_iota(jnp.int32, (rows, width), 0)
    whole = jnp.concatenate([piece[...] for piece in pieces], axis=1)
    out_ref[...] = jnp.where(pos < len_ref[0], whole, jnp.zeros_like(whole))


def place_rows(kernel, name, seq_rows, pieces, extra, scalars, buffer):
    tok_rows = pieces[0].shape[0]
    width = sum(piece.shape[1] for piece in pieces)
    count = len(scalars)
    whole = lambda item: pl.BlockSpec(item.shape, lambda i, *s: (0, 0))
    last = [] if buffer is None else [buffer]
    operands = list(pieces) + list(extra) + (last or [extra[0] if extra else pieces[0]])
    specs = [whole(item) for item in list(pieces) + list(extra)] + [pl.BlockSpec(memory_space=pl.ANY)]
    return pl.pallas_call(
        kernel,
        grid_spec=pltpu.PrefetchScalarGridSpec(
            num_scalar_prefetch=count,
            grid=(1,),
            in_specs=specs,
            out_specs=pl.BlockSpec((tok_rows, width), lambda i, at, *s: (at[0], 0)),
        ),
        out_shape=jax.ShapeDtypeStruct((seq_rows, width), BF16),
        input_output_aliases={count + len(operands) - 1: 0} if last else {},
        name=name,
    )(*scalars, *operands)


def sums_kernel(counts, at_ref, *refs):
    parts, (grad_ref, out_ref, gain_acc, shift_acc) = list(refs[:-4]), refs[-4:]
    rows = parts[0].shape[0]
    gain_acc[...] = jnp.zeros_like(gain_acc)
    shift_acc[...] = jnp.zeros_like(shift_acc)
    step = gain_acc.shape[0]
    for flip, count in enumerate(counts):
        pieces = [parts.pop(0) for _ in range(count)]
        base = pl.multiple_of((at_ref[0] ^ flip) * rows, rows)
        for low in range(0, rows, step):
            grad = grad_ref[pl.ds(base + low, step), :].astype(F32)
            gain_acc[...] += grad * norm_rows(joined(pieces, low, low + step))
            shift_acc[...] += grad
    out_ref[0:1, :] = jnp.sum(gain_acc[...], axis=0, keepdims=True)
    out_ref[1:2, :] = jnp.sum(shift_acc[...], axis=0, keepdims=True)


def norm_sums(tensor, parts, grad):
    width = grad.shape[1]
    pieces = [piece for part in parts for piece in part]
    vmem = pl.BlockSpec(memory_space=pltpu.VMEM)
    return pl.pallas_call(
        functools.partial(sums_kernel, [len(part) for part in parts]),
        in_specs=[pl.BlockSpec(memory_space=pltpu.SMEM)] + [vmem] * (len(pieces) + 1),
        out_specs=vmem,
        out_shape=jax.ShapeDtypeStruct((2, width), F32),
        scratch_shapes=[pltpu.VMEM((32, width), F32), pltpu.VMEM((32, width), F32)],
        compiler_params=pltpu.CompilerParams(vmem_limit_bytes=32 * 1024 * 1024),
        cost_estimate=pl.CostEstimate(flops=16 * grad.size, bytes_accessed=4 * grad.size, transcendentals=0),
        name="norm_sums",
    )(tensor, *pieces, grad)


def weight_kernel(at_ref, left_a, right_a, left_b, right_b, out_ref):
    width = right_a.shape[1]
    out_ref[:, :width] = inner_rows(left_a[...], right_a[...]).astype(BF16)
    out_ref[:, width:] = inner_rows(left_b[...], right_b[...]).astype(BF16)


def weight_grads(left_a, right_a, left_b, right_b, first, stride, blocks, rows):
    seq = left_a.shape[0]
    width = right_a.shape[1] + right_b.shape[1]
    block = pl.BlockSpec((seq, rows), lambda i, at: (0, stride * i + at[0]))
    whole = lambda item: pl.BlockSpec(item.shape, lambda i, at: (0, 0))
    return pl.pallas_call(
        weight_kernel,
        grid_spec=pltpu.PrefetchScalarGridSpec(
            num_scalar_prefetch=1,
            grid=(blocks,),
            in_specs=[block, whole(right_a), block, whole(right_b)],
            out_specs=pl.BlockSpec((rows, width), lambda i, at: (i, 0)),
        ),
        out_shape=jax.ShapeDtypeStruct((blocks * rows, width), BF16),
        compiler_params=pltpu.CompilerParams(vmem_limit_bytes=32 * 1024 * 1024),
        cost_estimate=pl.CostEstimate(
            flops=2 * seq * blocks * rows * width,
            bytes_accessed=2 * seq * (width + 2 * blocks * rows) + 2 * blocks * rows * width,
            transcendentals=0,
        ),
        name="weight_grads",
    )(first, left_a, right_a, left_b, right_b)


def tie(*values):
    return lax.optimization_barrier(values)


class LineScatter:
    def __init__(self, left_a, right_a, left_b, right_b):
        self.size = lax.axis_size("dp")
        self.stations = self.size // 2
        me = lax.axis_index("dp")
        self.core, self.place = me % 2, me // 2
        self.rows = left_a.shape[1] // self.size
        self.other = weight_grads(
            left_a, right_a, left_b, right_b, (1 - self.core)[None], 2, self.stations, self.rows
        )
        self.step = 0

    def finish_pair(self, left_a, right_a, left_b, right_b):
        self.mine = weight_grads(
            left_a, right_a, left_b, right_b, self.core[None], 2, self.stations, self.rows
        )
        self.held = (lax.ppermute(self.other, "dp", swap_pairs(self.size, 1)),)

    def at(self, target):
        target = jnp.clip(target, 0, self.stations - 1)
        pick = lambda item: lax.dynamic_slice_in_dim(item, target * self.rows, self.rows, 0).astype(F32)
        return pick(self.mine) + pick(self.got)

    def next_sends(self):
        if self.step == 0:
            (self.got,) = self.held
            self.held = (None, None)
        self.step += 1
        if self.step >= self.stations:
            up, down = self.held
            self.total = self.at(self.place) + up.astype(F32) + down.astype(F32)
            return ()
        up, down = self.held if len(self.held) == 2 else self.held * 2
        above = self.place + self.stations - self.step
        below = self.place - self.stations + self.step
        add = lambda sent, item: (sent if item is None else sent + item.astype(F32)).astype(BF16)
        if 2 * self.step < self.stations - 1:
            near = 2 * self.place < self.stations
            sent = self.at(jnp.where(near, above, below))
            return (add(sent, up),)
        return add(self.at(above), up), add(self.at(below), down)

    def send(self, sends):
        to_up = [(2 * z + c, 2 * z + 2 + c) for z in range(self.step) for c in range(2)]
        to_down = [(self.size - 1 - a, self.size - 1 - b) for a, b in to_up]
        if len(sends) == 1:
            self.held = (lax.ppermute(sends[0], "dp", to_up + to_down),)
        else:
            self.held = tuple(lax.ppermute(item, "dp", way) for item, way in zip(sends, (to_up, to_down)))

    def done(self):
        return self.step >= self.stations


def weave_kernel(at_ref, mine_ref, got_ref, out_ref):
    same = pl.program_id(0) % 2 == at_ref[1]

    @pl.when(same)
    def _():
        out_ref[...] = mine_ref[...]

    @pl.when(jnp.logical_not(same))
    def _():
        out_ref[...] = got_ref[...]


class LineGather:
    def __init__(self, pack):
        self.size = lax.axis_size("dp")
        self.stations = self.size // 2
        me = lax.axis_index("dp")
        self.core, self.place = me % 2, me // 2
        self.pack = pack
        self.step = 1
        self.came = []
        self.send((pack, pack))

    def send(self, sends):
        if self.step == self.stations:
            self.held = (lax.ppermute(sends[0], "dp", swap_pairs(self.size, 1)),)
            return
        to_up = [(2 * z + c, 2 * z + 2 + c) for z in range(self.step - 1, self.stations - 1) for c in range(2)]
        to_down = [(self.size - 1 - a, self.size - 1 - b) for a, b in to_up]
        if len(sends) == 1:
            self.held = (lax.ppermute(sends[0], "dp", to_up + to_down),)
        else:
            self.held = tuple(lax.ppermute(item, "dp", way) for item, way in zip(sends, (to_up, to_down)))

    def next_sends(self):
        self.step += 1
        if self.step == self.stations + 1:
            self.full = self.weave(self.stack, self.held[0])
            return ()
        up, down = self.held if len(self.held) == 2 else self.held * 2
        self.came.append((up, down))
        if self.step == self.stations:
            parts = [self.pack]
            for far in range(1, self.stations):
                ahead = self.place + far < self.stations
                parts.append(jnp.where(ahead, self.came[far - 1][1], self.came[self.stations - far - 1][0]))
            self.stack = jnp.concatenate(parts)
            return (self.stack,)
        if 2 * self.step > self.stations + 1:
            return (jnp.where(2 * self.place >= self.stations, up, down),)
        return up, down

    def weave(self, mine, got):
        rows, width = self.pack.shape
        stations = self.stations
        half = pl.BlockSpec((rows, width), lambda i, at: ((i // 2 + stations - at[0]) % stations, 0))
        return pl.pallas_call(
            weave_kernel,
            grid_spec=pltpu.PrefetchScalarGridSpec(
                num_scalar_prefetch=1,
                grid=(self.size,),
                in_specs=[half, half],
                out_specs=pl.BlockSpec((rows, width), lambda i, at: (i, 0)),
            ),
            out_shape=jax.ShapeDtypeStruct((self.size * rows, width), BF16),
            cost_estimate=pl.CostEstimate(
                flops=0, bytes_accessed=6 * self.size * rows * width, transcendentals=0
            ),
            name="weave",
        )(jnp.stack([self.place, self.core]).astype(jnp.int32), mine, got)

    def done(self):
        return self.step > self.stations


def advance(lines, *values):
    lines = [line for line in lines if not line.done()]
    flat = tie(*[item for line in lines for item in line.held], *values)
    for line in lines:
        line.held, flat = flat[: len(line.held)], flat[len(line.held) :]
    sends = [line.next_sends() for line in lines]
    flat = tie(*[item for sent in sends for item in sent], *flat)
    for line, sent in zip(lines, sends):
        if sent:
            line.send(flat[: len(sent)])
            flat = flat[len(sent) :]
    return flat


def natural_grads(left_a, right_a, left_b, right_b):
    size = lax.axis_size("dp")
    zero = jnp.zeros((1,), jnp.int32)
    return weight_grads(left_a, right_a, left_b, right_b, zero, 1, size, left_a.shape[1] // size)


class TensorScatter:
    def __init__(self, partial, tok_rows):
        self.count = lax.axis_size("tensor")
        tensor = lax.axis_index("tensor")
        half = partial.shape[1] // 2

        def block(flip, side):
            start = ((tensor ^ flip) * tok_rows, side * half)
            return lax.dynamic_slice(partial, start, (tok_rows, half))

        self.block, self.tok_rows = block, tok_rows
        self.rest = []
        if self.count > 4:
            self.rest = [
                lax.ppermute(block(flip, side), "tensor", swap_pairs(self.count, flip))
                for side in (0, 1)
                for flip in range(1, self.count)
            ]
            return
        self.first = []
        for side, flip in ((0, 1), (1, 2)):
            sent = jnp.concatenate([block(flip, side), block(3, side)])
            self.first.append(lax.ppermute(sent, "tensor", swap_pairs(self.count, flip)))

    def second(self, *values):
        if self.count > 4:
            return values
        self.total = []
        flat = tie(*self.first, *values)
        self.first, values = flat[:2], flat[2:]
        for side, flip in ((0, 1), (1, 2)):
            got = self.first[side].astype(F32)
            far = (self.block(3 - flip, side).astype(F32) + got[self.tok_rows :]).astype(BF16)
            near = self.block(0, side).astype(F32) + got[: self.tok_rows]
            self.total.append((near, lax.ppermute(far, "tensor", swap_pairs(self.count, 3 - flip))))
        return values

    def result(self, *values):
        if self.count > 4:
            flat = tie(*self.rest, *values)
            many = self.count - 1
            total = [
                sum((item.astype(F32) for item in flat[side * many : (side + 1) * many]), self.block(0, side).astype(F32))
                for side in (0, 1)
            ]
            return (jnp.concatenate(total, axis=1),) + flat[2 * many :]
        flat = tie(*[item for _, item in self.total], *values)
        total = [near + item.astype(F32) for (near, _), item in zip(self.total, flat)]
        return (jnp.concatenate(total, axis=1),) + flat[2:]


def all_sum(value, axis):
    count = lax.axis_size(axis)
    for bit in bits_below(count):
        value = value + lax.ppermute(value, axis, swap_pairs(count, bit))
    return value


def gelu_pair(value):
    slope = (2.0 / jnp.pi) ** 0.5
    square = value * value
    flat = jnp.tanh(slope * value * (1.0 + 0.044715 * square))
    act = 0.5 * value * (1.0 + flat)
    back = 0.5 * (1.0 + flat) + 0.5 * value * (1.0 - flat * flat) * slope * (1.0 + 3 * 0.044715 * square)
    return act.astype(BF16), back.astype(BF16)


def on_device(
    tokens,
    cotangent,
    lengths,
    norm_gain,
    norm_bias,
    query_weight,
    key_weight,
    value_weight,
    qkv_bias,
    proj_weight,
    proj_bias,
    up_weight,
    up_bias,
    down_weight,
    down_bias,
):
    tensor_count = lax.axis_size("tensor")
    dp_count = lax.axis_size("dp")
    tensor = lax.axis_index("tensor")
    place = lax.axis_index("dp")
    tok_rows, width = tokens.shape
    seq_rows = tok_rows * tensor_count
    heads_width = query_weight.shape[1]
    ff = up_weight.shape[1]
    pairs = heads_width // LANES
    slot_len = lengths[0]

    small = jnp.concatenate(
        [norm_gain, norm_bias, proj_bias, down_bias, qkv_bias.reshape(-1), up_bias.reshape(-1)]
    )
    mine_row = (jnp.arange(dp_count) == place)[:, None]
    small_all = all_sum(jnp.where(mine_row, small[None, :], jnp.zeros((), BF16)), "dp")
    shard = norm_gain.shape[0]
    b_out = (
        small_all[:, 2 * shard : 3 * shard].astype(F32) + small_all[:, 3 * shard : 4 * shard].astype(F32)
    ).reshape(-1)
    heads_here = qkv_bias.shape[1]
    head_size = qkv_bias.size
    b_heads = (
        small_all[:, 4 * shard : 4 * shard + head_size]
        .reshape((dp_count,) + qkv_bias.shape)
        .transpose(1, 2, 0, 3)
        .reshape(3, pairs, LANES)
    )
    b_qkv = b_heads.transpose(1, 0, 2).reshape(-1).astype(F32)
    b_up = (
        small_all[:, 4 * shard + head_size :]
        .reshape((dp_count,) + up_bias.shape)
        .transpose(1, 0, 2)
        .reshape(-1)
        .astype(F32)
    )

    down_t = down_weight.T
    weight_sum = sum(MLP_PARTS)
    edges = [0]
    for part in MLP_PARTS:
        edges.append(edges[-1] + ff * part // weight_sum)

    def mlp_pack(index):
        low, high = edges[index], edges[index + 1]
        return jnp.concatenate([up_weight[:, low:high], down_t[:, low:high]], axis=1)

    attn_in = [
        item[:, p * LANES : (p + 1) * LANES]
        for p in range(pairs)
        for item in (query_weight, key_weight, value_weight)
    ]
    attn_pack = jnp.concatenate(attn_in + [proj_weight.T], axis=1)
    attn_full = lax.all_gather(attn_pack, "dp", axis=0, tiled=True)
    near_pack, far_pack = mlp_pack(0), mlp_pack(1)

    half = width // 2

    def direct(rows, flip):
        return lax.ppermute(rows, "tensor", swap_pairs(tensor_count, flip))

    def third(first, second):
        return [direct(first[:, :half], 2), direct(second[:, half:], 1)]

    tok_one, tok_two, small_all = tie(direct(tokens, 1), direct(tokens, 2), small_all)
    tok_one, near_pack = tie(tok_one, near_pack)
    near_full = lax.all_gather(near_pack, "dp", axis=0, tiled=True)
    tok_three = third(tok_one, tok_two)
    cot_held, tok_one, tok_two = tie(cotangent, tok_one, tok_two)
    cot_one, cot_two = direct(cot_held, 1), direct(cot_held, 2)
    more = range(4, tensor_count)
    tok_more = [[direct(tokens, flip)] for flip in more]

    n_gain = small_all[:, :shard].reshape(-1).astype(F32)
    n_shift = small_all[:, shard : 2 * shard].reshape(-1).astype(F32)

    def where_of(flip):
        return (tensor ^ flip).astype(jnp.int32)[None]

    gain_row, shift_row = n_gain[None, :], n_shift[None, :]
    tok_parts = [[tokens], [tok_one], [tok_two], tok_three] + tok_more
    normed = None
    for flip in range(tensor_count):
        if flip == 3:
            normed, cot_one, cot_two = tie(normed, cot_one, cot_two)
            cot_three = third(cot_one, cot_two)
        normed = place_rows(
            norm_kernel, "norm_rows", seq_rows, tok_parts[flip], [gain_row, shift_row], [where_of(flip)], normed
        )
    cot_parts = [[cotangent], [cot_one], [cot_two], cot_three] + [[direct(cot_held, flip)] for flip in more]
    grad_all = None
    for flip in range(tensor_count):
        grad_all = place_rows(
            mask_kernel, "mask_rows", seq_rows, cot_parts[flip], [], [where_of(flip), lengths], grad_all
        )
    normed, grad_all, far_pack = tie(normed, grad_all, far_pack)

    tables = rotary_lanes(seq_rows)
    in_cols = 3 * heads_width
    w_qkv = attn_full[:, :in_cols]
    w_proj_t = attn_full[:, in_cols:]
    qkv = product(normed, w_qkv) + b_qkv
    q_low, k_low, v_low, mixed, lse = attention_forward(lengths, qkv, tables)
    mixed_grad = product(grad_all, w_proj_t).astype(BF16)
    qkv_grad = attention_backward(lengths, q_low, k_low, v_low, mixed_grad, lse, tables)
    head_bias_grad = jnp.sum(qkv_grad, axis=0, dtype=F32)
    attn_line = LineScatter(normed, qkv_grad, grad_all, mixed)
    qkv_grad, mixed, attn_line.other = tie(qkv_grad, mixed, attn_line.other)
    attn_line.finish_pair(normed, qkv_grad, grad_all, mixed)
    far_pack, attn_line.mine = tie(far_pack, attn_line.mine)
    gather = LineGather(far_pack)
    near_full, normed, attn_line.mine = tie(near_full, normed, attn_line.mine)

    def forward(full, low, high):
        w_up, w_down_t = full[:, : high - low], full[:, high - low :]
        act, back = tie(*gelu_pair(product(normed, w_up) + b_up[low:high]))
        return w_up, w_down_t, act, back

    def plus(total, left, right):
        return (total.astype(F32) + times_trans(left, right)).astype(BF16)

    near_up, near_down_t, near_act, back = forward(near_full, edges[0], edges[1])
    near_grad = (product(grad_all, near_down_t) * back.astype(F32)).astype(BF16)
    near_act, near_grad, grad_all = advance([attn_line, gather], near_act, near_grad, grad_all)
    line = LineScatter(normed, near_grad, grad_all, near_act)
    near_act, near_grad, line.other = tie(near_act, near_grad, line.other)
    line.finish_pair(normed, near_grad, grad_all, near_act)
    near_act, line.mine, mixed, qkv_grad = advance(
        [attn_line, gather], near_act, line.mine, mixed, qkv_grad
    )
    branch = times_trans(mixed, w_proj_t).astype(BF16)
    normed_grad = times_trans(qkv_grad, w_qkv).astype(BF16)
    branch, normed_grad, near_act = advance([gather, line], branch, normed_grad, near_act)
    branch = plus(branch, near_act, near_down_t)
    lines = [attn_line, line]
    branch, normed, grad_all, near_grad = advance([gather, attn_line], branch, normed, grad_all, near_grad)
    while not gather.done():
        normed, grad_all = advance([gather], normed, grad_all)
    w_up, w_down_t, act, back = forward(gather.full, edges[1], edges[2])
    up_pre_grad = (product(grad_all, w_down_t) * back.astype(F32)).astype(BF16)
    up_pre_grad, act, grad_all = advance([line], up_pre_grad, act, grad_all)
    far_grad = natural_grads(normed, up_pre_grad, grad_all, act)
    far_grad, act, up_pre_grad, near_grad = advance([attn_line], far_grad, act, up_pre_grad, near_grad)
    far_shard = lax.psum_scatter(far_grad, "dp", scatter_dimension=0, tiled=True)
    branch_low = plus(branch, act, w_down_t)

    output_sum = TensorScatter(branch_low, tok_rows)
    near_grad, branch_low = advance([line], near_grad, branch_low)
    normed_grad_low = plus(plus(normed_grad, near_grad, near_up), up_pre_grad, w_up)
    (normed_grad_low,) = output_sum.second(normed_grad_low)
    up_bias_grads = [jnp.sum(item, axis=0, dtype=F32) for item in (near_grad, up_pre_grad)]
    grad_sum = TensorScatter(normed_grad_low, tok_rows)
    (normed_grad_low,) = advance(lines, normed_grad_low)
    gain_shift = norm_sums(tensor.astype(jnp.int32)[None], tok_parts, normed_grad_low)
    (gain_shift,) = grad_sum.second(gain_shift)
    own = tokens.astype(F32)
    (output_rows,) = output_sum.result()
    output = (own + output_rows + b_out).astype(BF16)
    own_pos = tensor * tok_rows + jnp.arange(tok_rows)
    own_grad = jnp.where((own_pos < slot_len)[:, None], cotangent.astype(F32), 0.0)

    shared = jnp.concatenate([gain_shift.reshape(-1), jnp.sum(own_grad, axis=0)])
    kept = jnp.concatenate([head_bias_grad] + up_bias_grads)
    shared = all_sum(shared.reshape(-1, LANES), "tensor")
    while not all(item.done() for item in lines):
        (shared,) = advance(lines, shared)
    many = shared.shape[0]
    summed = jnp.concatenate([shared, kept.reshape(-1, LANES)])
    attn_shard = attn_line.total
    mlp_shards = [line.total, far_shard.astype(F32)]
    up_out = jnp.concatenate([item[:, : item.shape[1] // 2] for item in mlp_shards], axis=1)
    down_out = jnp.concatenate([item[:, item.shape[1] // 2 :].T for item in mlp_shards], axis=0)
    (own_normed_grad,) = grad_sum.result()
    _, norm_back = jax.vjp(lambda rows: layer_norm(rows, n_gain, n_shift), own)
    input_grad = own_grad + norm_back(own_normed_grad)[0]
    summed, input_grad, up_out, down_out = tie(summed, input_grad, up_out, down_out)
    summed = all_sum(summed, "dp")
    shared = summed[:many].reshape(3, dp_count, shard)
    gain_grad, shift_grad, out_bias = lax.dynamic_index_in_dim(shared, place, 1, keepdims=False)
    kept = summed[many:].reshape(-1)
    head_out = lax.dynamic_index_in_dim(
        kept[: head_bias_grad.shape[0]]
        .reshape(pairs, 3, LANES)
        .transpose(1, 0, 2)
        .reshape(3, heads_here, dp_count, HEAD // dp_count),
        place,
        2,
        keepdims=False,
    )
    up_bias_out = lax.dynamic_index_in_dim(
        kept[head_bias_grad.shape[0] :].reshape(up_bias.shape[0], dp_count, -1), place, 1, keepdims=False
    )

    def part_of(which):
        return jnp.concatenate(
            [attn_shard[:, (3 * p + which) * LANES : (3 * p + which + 1) * LANES] for p in range(pairs)], axis=1
        )

    return (
        output,
        input_grad,
        gain_grad,
        shift_grad,
        part_of(0),
        part_of(1),
        part_of(2),
        head_out,
        attn_shard[:, in_cols:].T,
        out_bias,
        up_out,
        up_bias_out,
        down_out,
        out_bias,
    )


def solution(mesh):
    rows = P(("dp", "tensor"), None)
    both = P("dp", "tensor")
    turned = P("tensor", "dp")
    heads = P(None, "tensor", "dp")
    vec = P("dp")
    return jax.shard_map(
        on_device,
        mesh=mesh,
        in_specs=(rows, rows, vec, vec, vec, both, both, both, heads, turned, vec, both, turned, turned, vec),
        out_specs=(rows, rows, vec, vec, both, both, both, heads, turned, vec, both, turned, turned, vec),
        check_vma=False,
    )
```
